32 devices in a mesh: batch: 8 (over y, x, core), seq: 4 (over z).
Axes of the slice: x: 2, y: 2, z: 4, core: 2. Of those that a mesh axis runs over, the one named last changes fastest.
Arguments:
- inputs: bfloat16 [16, 512, 1536], P('batch', 'seq'), may hold values from -6 to 6
- output_grad: bfloat16 [16, 512, 1536], P('batch', 'seq'), may hold values from -6 to 6
- source_tags: int32 [16], P('batch'), may hold values from 0 to 7
- source_counts: int32 [8], replicated, may hold values from 256 to 1023
- gain_in: bfloat16 [1536], P(('batch', 'seq')), may hold values from 0.099609375 to 1.8984375
- w_query: bfloat16 [1536, 1536], P(('batch', 'seq')), may hold values from -0.15625 to 0.15625
- w_key: bfloat16 [1536, 1536], P(('batch', 'seq')), may hold values from -0.15625 to 0.15625
- w_value: bfloat16 [1536, 1536], P(('batch', 'seq')), may hold values from -0.15625 to 0.15625
- kernel: float32 [16, 6, 11], replicated, may hold values from -1.25 to 1.25
- mixing: float32 [16, 2], replicated, may hold values from 0.25 to 1.25
- gain_head: bfloat16 [1536], P(('batch', 'seq')), may hold values from 0.099609375 to 1.8984375
- w_out: bfloat16 [1536, 1536], P(('batch', 'seq')), may hold values from -0.15625 to 0.15625
- gain_mid: bfloat16 [1536], P(('batch', 'seq')), may hold values from 0.099609375 to 1.8984375
- w_gate: bfloat16 [1536, 4096], P('batch', 'seq'), may hold values from -0.15625 to 0.15625
- w_up: bfloat16 [1536, 4096], P('batch', 'seq'), may hold values from -0.15625 to 0.15625
- w_down: bfloat16 [4096, 1536], P('seq', 'batch'), may hold values from -0.09375 to 0.09375
Outputs:
- output: bfloat16 [16, 512, 1536], P('batch', 'seq')
- input_grad: bfloat16 [16, 512, 1536], P('batch', 'seq')
- grad_gain_in: float32 [1536], P(('batch', 'seq'))
- grad_query: float32 [1536, 1536], P(('batch', 'seq'))
- grad_key: float32 [1536, 1536], P(('batch', 'seq'))
- grad_value: float32 [1536, 1536], P(('batch', 'seq'))
- grad_kernel: float32 [16, 6, 11], replicated
- grad_mixing: float32 [16, 2], replicated
- grad_gain_head: float32 [1536], P(('batch', 'seq'))
- grad_out: float32 [1536, 1536], P(('batch', 'seq'))
- grad_gain_mid: float32 [1536], P(('batch', 'seq'))
- grad_gate: float32 [1536, 4096], P('batch', 'seq')
- grad_up: float32 [1536, 4096], P('batch', 'seq')
- grad_down: float32 [4096, 1536], P('seq', 'batch')
The draws below stay inside these ranges and needn't reach their ends.
All inputs are finite; a program needn't handle non-finite values.
Results may differ from the reference program's by a relative error of at most 0.018.
The reference program's roundings to bfloat16 on the way count: a program that leaves them out, or rounds other values in their place, can miss the bound.
Values may be sent and summed in bfloat16 or wider, within the bound.
No kernel may reach another device: no remote copies, remote signals or barrier semaphores. Data moves between devices by JAX's collectives and lax.ppermute only.
A program may use at most 384 MiB of HBM per device.

```python
import math
import jax
import jax.numpy as jnp
from jax import lax

D = 1536
H = 16
DH = 96
FF = 4096
QUERY_TAPS = 6
KEY_TAPS = 11
SOURCES = 8
SEQS = 16
LEN = 512


def set_ends(array, rng, least, high):
    longest = array.shape.index(max(array.shape))
    spots = []
    for shift in (0, 1):
        where = [jax.random.randint(jax.random.fold_in(rng, axis), (), 0, length) for axis, length in enumerate(array.shape)]
        where[longest] = (where[longest] + shift) % array.shape[longest]
        spots.append(tuple(where))
    return array.at[spots[0]].set(least).at[spots[1]].set(high)


def level_of(own_key, dims, cuts, low, largest):
    factor_of = 1.0
    for dim, blocks in cuts:
        steps = jax.random.uniform(jax.random.fold_in(jax.random.fold_in(own_key, 6), dim), (blocks,), jnp.float32, low / len(cuts), largest / len(cuts))
        factor_of = factor_of * jnp.repeat(jnp.exp(steps), dims[dim] // blocks).reshape((-1,) + (1,) * (len(dims) - 1 - dim))
    return factor_of


def scatter_about(rng, shape, width, most, cuts=(), kind=jnp.bfloat16):
    array = width * jax.random.normal(rng, shape, jnp.float32)
    if cuts:
        array = array * level_of(rng, shape, cuts, -0.22, 0.18)
    return jnp.clip(array, -most, most).astype(kind)


def setup_inputs(seed: int = 0) -> dict:
    keys = jax.random.split(jax.random.key(seed), 17)
    return {
        "inputs": scatter_about(keys[0], (SEQS, LEN, D), 1.0, 6.0, ((0, 8), (1, 4))),
        "output_grad": scatter_about(keys[1], (SEQS, LEN, D), 1.0, 6.0, ((0, 8), (1, 4))),
        "source_tags": set_ends(jax.random.randint(keys[2], (SEQS,), 0, SOURCES), jax.random.fold_in(keys[2], 1), 0, SOURCES - 1).astype(jnp.int32),
        "source_counts": set_ends(jax.random.randint(keys[3], (SOURCES,), LEN // 2, 2 * LEN), jax.random.fold_in(keys[3], 1), LEN // 2, (2 * LEN) - 1).astype(jnp.int32),
        "gain_in": jnp.clip(1.0 + 0.18 * jax.random.normal(keys[4], (D,), jnp.float32), 0.099609375, 1.8984375).astype(jnp.bfloat16),
        "w_query": scatter_about(keys[5], (D, D), D ** -0.5, 0.15625, ((0, 32),)),
        "w_key": scatter_about(keys[6], (D, D), D ** -0.5, 0.15625, ((0, 32),)),
        "w_value": scatter_about(keys[7], (D, D), D ** -0.5, 0.15625, ((0, 32),)),
        "kernel": scatter_about(keys[8], (H, QUERY_TAPS, KEY_TAPS), 0.2, 1.25, (), jnp.float32),
        "mixing": jnp.clip(jax.random.uniform(keys[9], (H, 2), jnp.float32, 0.25, 1.25), 0.25, 1.25),
        "gain_head": jnp.clip(1.0 + 0.18 * jax.random.normal(keys[10], (D,), jnp.float32), 0.099609375, 1.8984375).astype(jnp.bfloat16),
        "w_out": scatter_about(keys[11], (D, D), D ** -0.5, 0.15625, ((0, 32),)),
        "gain_mid": jnp.clip(1.0 + 0.18 * jax.random.normal(keys[12], (D,), jnp.float32), 0.099609375, 1.8984375).astype(jnp.bfloat16),
        "w_gate": scatter_about(keys[13], (D, FF), D ** -0.5, 0.15625, ((0, 8), (1, 4))),
        "w_up": scatter_about(keys[14], (D, FF), D ** -0.5, 0.15625, ((0, 8), (1, 4))),
        "w_down": scatter_about(keys[15], (FF, D), FF ** -0.5, 0.09375, ((0, 4), (1, 8))),
    }


@jax.custom_vjp
def low(v):
    return lax.optimization_barrier(v.astype(jnp.bfloat16)).astype(jnp.float32)

@jax.custom_vjp
def low_back(v):
    return v

def low_keep(v):
    return (low(v), None)

def low_pass(kept, grad):
    return (grad,)

def back_keep(v):
    return (v, None)

def back_low(kept, grad):
    return (low(grad),)
low.defvjp(low_keep, low_pass)
low_back.defvjp(back_keep, back_low)
highest = lax.Precision.HIGHEST

def matmul(left, right):
    return jnp.dot(left, right, preferred_element_type=jnp.float32, precision=highest)

def rms_scale(values, gain):
    return values * lax.rsqrt(lax.optimization_barrier(jnp.mean(values * values, axis=-1, keepdims=True)) + 1e-06) * gain

def head_norm(values, gain):
    row_count = values.shape[0]
    grouped = values.reshape(row_count, H, DH)
    centred = grouped - lax.optimization_barrier(jnp.mean(grouped, axis=-1, keepdims=True))
    spread = lax.optimization_barrier(jnp.mean(centred * centred, axis=-1, keepdims=True))
    return (centred * lax.rsqrt(spread + 1e-05)).reshape(row_count, H * DH) * gain

def mixed_probs(raw_scores, kernel_pair, mixing_pair, first_row):
    rim = QUERY_TAPS - 1
    reach = KEY_TAPS // 2
    row_count = raw_scores.shape[1] - rim
    key_count = raw_scores.shape[2]
    key_pos = jnp.arange(key_count, dtype=jnp.int32)[None, :]
    query_pos = jnp.arange(row_count + rim, dtype=jnp.int32)[:, None] + (first_row - rim)
    masked = jnp.where(key_pos <= query_pos, raw_scores, 0.0)
    padded = jnp.pad(masked, ((0, 0), (0, 0), (reach, reach)))
    total = jnp.zeros((2, row_count, key_count), raw_scores.dtype)
    for row_lag in range(QUERY_TAPS):
        for key_lag in range(KEY_TAPS):
            window = padded[:, rim - row_lag:rim - row_lag + row_count, 2 * reach - key_lag:2 * reach - key_lag + key_count]
            total = total + kernel_pair[:, row_lag, key_lag][:, None, None] * window
    valid = key_pos <= query_pos[rim:]
    filled = jnp.where(valid, total, -1e+30)
    top = lax.optimization_barrier(jnp.max(filled, axis=-1, keepdims=True))
    expon = jnp.where(valid, jnp.exp(filled - top), 0.0)
    probs = expon / lax.optimization_barrier(jnp.sum(expon, axis=-1, keepdims=True))
    return mixing_pair[:, 0][:, None, None] * probs[0][None] + mixing_pair[:, 1][:, None, None] * probs[1][None]

def attend_block(query_ext, key_block, value_block, kernel_pair, mixing_pair):
    scale = 1.0 / math.sqrt(DH)
    scores = jnp.einsum('qhd,khd->hqk', query_ext, key_block, precision=highest) * scale
    raw_scores = low_back(scores)
    mixed = low(mixed_probs(raw_scores, kernel_pair, mixing_pair, 0))
    return jnp.einsum('hqk,khd->qhd', mixed, value_block, precision=highest)

def split_groups(values):
    shaped = values.reshape(SEQS, LEN, H // 2, 2, DH).transpose(0, 2, 1, 3, 4)
    return shaped.reshape(SEQS * (H // 2), LEN, 2, DH)

def attention(queries, keys_all, values_all, kernel, mixing):
    rim = QUERY_TAPS - 1
    query_blocks = jnp.pad(split_groups(queries), ((0, 0), (rim, 0), (0, 0), (0, 0)))
    kernel_blocks = jnp.broadcast_to(kernel.reshape(1, H // 2, 2, QUERY_TAPS, KEY_TAPS), (SEQS, H // 2, 2, QUERY_TAPS, KEY_TAPS)).reshape(SEQS * (H // 2), 2, QUERY_TAPS, KEY_TAPS)
    mixing_blocks = jnp.broadcast_to(mixing.reshape(1, H // 2, 2, 2), (SEQS, H // 2, 2, 2)).reshape(SEQS * (H // 2), 2, 2)
    guarded = jax.checkpoint(attend_block)

    def one_block(packed):
        return guarded(packed[0], packed[1], packed[2], packed[3], packed[4])
    blocks = lax.map(one_block, (query_blocks, split_groups(keys_all), split_groups(values_all), kernel_blocks, mixing_blocks))
    return blocks.reshape(SEQS, H // 2, LEN, 2, DH).transpose(0, 2, 1, 3, 4).reshape(SEQS * LEN, H * DH)

def forward(inputs, gain_in, w_query, w_key, w_value, kernel, mixing, gain_head, w_out, gain_mid, w_gate, w_up, w_down):
    normed = low(rms_scale(inputs, gain_in))
    queries = low(low_back(matmul(normed, w_query)))
    keys_all = low(low_back(matmul(normed, w_key)))
    values_all = low(low_back(matmul(normed, w_value)))
    heads = low_back(attention(queries, keys_all, values_all, kernel, mixing))
    joined = low(head_norm(heads, gain_head))
    middle = inputs + low_back(matmul(joined, w_out))
    normed_mid = low(rms_scale(middle, gain_mid))
    gate = low_back(matmul(normed_mid, w_gate))
    upward = low_back(matmul(normed_mid, w_up))
    hidden = low(jax.nn.silu(gate) * upward)
    return middle + low_back(matmul(hidden, w_down))

def reference(inputs, output_grad, source_tags, source_counts, gain_in, w_query, w_key, w_value, kernel, mixing, gain_head, w_out, gain_mid, w_gate, w_up, w_down):
    flat_inputs = inputs.reshape(SEQS * LEN, D)
    floats = (flat_inputs, gain_in, w_query, w_key, w_value, kernel, mixing, gain_head, w_out, gain_mid, w_gate, w_up, w_down)
    floats = tuple((item.astype(jnp.float32) for item in floats))
    result, pullback = jax.vjp(forward, *floats)
    seq_scale = LEN / source_counts[source_tags].astype(jnp.float32)
    cotangent = (output_grad.astype(jnp.float32) * seq_scale[:, None, None]).reshape(SEQS * LEN, D)
    grads = pullback(cotangent)
    output = result.reshape(SEQS, LEN, D).astype(jnp.bfloat16)
    input_grad = grads[0].reshape(SEQS, LEN, D).astype(jnp.bfloat16)
    return (output, input_grad, grads[1], grads[2], grads[3], grads[4], grads[5], grads[6], grads[7], grads[8], grads[9], grads[10], grads[11], grads[12])
```

```python
import math

import jax
import jax.numpy as jnp
from jax import lax
from jax.experimental import pallas as pl
from jax.experimental.pallas import tpu as pltpu
from jax.sharding import PartitionSpec as P

H = 16
DH = 96
QT = 6
KT = 11
REACH = KT // 2
TILE = 128
PAIR = 256
PAD = 16
bf16 = jnp.bfloat16
f32 = jnp.float32


def nn(a, b):
    return lax.dot_general(a, b, (((1,), (0,)), ((), ())), preferred_element_type=f32)


def nt(a, b):
    return lax.dot_general(a, b, (((1,), (1,)), ((), ())), preferred_element_type=f32)


def tn(a, b):
    return lax.dot_general(a, b, (((0,), (0,)), ((), ())), preferred_element_type=f32)


def head_lanes(head, width=PAIR):
    lane = lax.broadcasted_iota(jnp.int32, (1, width), 1)
    return jnp.logical_and(lane >= head * DH, lane < (head + 1) * DH).astype(f32)


def split(value):
    high = value.astype(bf16)
    return high, (value - high.astype(f32)).astype(bf16)


def fill_bands(kern_ref, base, bands, low_bands, offset):
    row = lax.broadcasted_iota(jnp.int32, (2 * TILE, TILE), 0)
    col = lax.broadcasted_iota(jnp.int32, (2 * TILE, TILE), 1)
    tap = offset(row, col)
    for lag in range(QT):
        band = jnp.zeros((2 * TILE, TILE), f32)
        for key_lag in range(KT):
            band = jnp.where(tap == key_lag, kern_ref[base + lag * KT + key_lag], band)
        high, low = split(band)
        bands[:, lag * TILE : (lag + 1) * TILE] = high
        if low_bands is not None:
            low_bands[:, lag * TILE : (lag + 1) * TILE] = low


def valid_keys(first_query, rows, first_key):
    query = lax.broadcasted_iota(jnp.int32, (rows, TILE), 0) + first_query
    key = lax.broadcasted_iota(jnp.int32, (rows, TILE), 1) + (first_key - REACH)
    return jnp.logical_and(key >= 0, key <= query)


def shift_keys(keys, kx_ref):
    moved = jnp.concatenate([keys.astype(f32), jnp.zeros((TILE, PAIR), f32)], axis=0)
    kx_ref[...] = pltpu.roll(moved, REACH, 0).astype(bf16)


def norm_parts(heads):
    means = jnp.zeros_like(heads)
    masks = [head_lanes(0), head_lanes(1)]
    for mask in masks:
        means = means + mask * (jnp.sum(heads * mask, axis=1, keepdims=True) / DH)
    used = masks[0] + masks[1]
    centred = (heads - means) * used
    inverse = jnp.zeros_like(heads)
    for mask in masks:
        spread = jnp.sum(centred * centred * mask, axis=1, keepdims=True) / DH
        inverse = inverse + mask * lax.rsqrt(spread + 1e-05)
    return centred, inverse, masks


def attend_fwd_body(kern_ref, mix_ref, qkv_ref, gain_ref, joined_ref, heads_ref, p_ref, high_ref, low_ref, bands_ref, low_bands_ref, kx_ref):
    length = qkv_ref.shape[1]
    tiles = length // TILE
    scale = 1.0 / math.sqrt(DH)
    group = pl.program_id(0)

    @pl.when(jnp.logical_and(group == 0, pl.program_id(1) == 0))
    def _():
        high_ref[...] = jnp.zeros_like(high_ref)
        low_ref[...] = jnp.zeros_like(low_ref)

    shift_keys(qkv_ref[0, :, PAIR : 2 * PAIR], kx_ref)

    def one_head(head, carry):
        base = (group * 2 + head) * (QT * KT)
        fill_bands(kern_ref, base, bands_ref, low_bands_ref, lambda row, col: (KT - 1) - (row - col))
        lanes = head_lanes(head).astype(bf16)
        query = qkv_ref[0, :, :PAIR] * lanes
        for tile in range(tiles + 1):
            first = max(0, tile * TILE - PAD)
            scores = nt(query[first:], kx_ref[tile * TILE : (tile + 1) * TILE, :]) * scale
            masked = jnp.where(valid_keys(first, length - first, tile * TILE), scores, 0.0)
            high, low = split(masked)
            high_ref[first + PAD :, tile * TILE : (tile + 1) * TILE] = high
            low_ref[first + PAD :, tile * TILE : (tile + 1) * TILE] = low
        for tile in range(tiles):
            first = tile * TILE
            high = high_ref[first:, first : first + 2 * TILE]
            low = low_ref[first:, first : first + 2 * TILE]
            bands = bands_ref[...]
            wide = nn(high, bands) + nn(low, bands) + nn(high, low_bands_ref[...])
            total = wide[:, :TILE]
            for lag in range(1, QT):
                total = total + pltpu.roll(wide[:, lag * TILE : (lag + 1) * TILE], lag, 0)
            p_ref[0, 0, head, first:, first : first + TILE] = total[PAD:]
        return carry

    lax.fori_loop(0, 2, one_head, 0)
    for tile in range(tiles):
        first = tile * TILE
        span = first + TILE
        query = lax.broadcasted_iota(jnp.int32, (TILE, span), 0) + first
        key = lax.broadcasted_iota(jnp.int32, (TILE, span), 1)
        valid = key <= query
        probs = []
        for head in range(2):
            logits = jnp.where(valid, p_ref[0, 0, head, first:span, :span], -1e30)
            top = jnp.max(logits, axis=1, keepdims=True)
            expon = jnp.where(valid, jnp.exp(logits - top), 0.0)
            prob = expon / jnp.sum(expon, axis=1, keepdims=True)
            p_ref[0, 0, head, first:span, :span] = prob
            probs.append(prob)
        out = jnp.zeros((TILE, PAIR), f32)
        for head in range(2):
            spot = (group * 2 + head) * 2
            mixed = (mix_ref[spot] * probs[0] + mix_ref[spot + 1] * probs[1]).astype(bf16)
            out = out + nn(mixed, qkv_ref[0, :span, 2 * PAIR :] * head_lanes(head).astype(bf16))
        heads_ref[0, first:span, :] = out
        centred, inverse, _ = norm_parts(out)
        joined_ref[0, first:span, :] = (centred * inverse * gain_ref[...]).astype(bf16)


def attend_bwd_body(kern_ref, mix_ref, qkv_ref, gain_ref, heads_ref, p_ref, dj_ref, dqkv_ref, gk_ref, gmix_ref, ggain_ref, d_ref, dlow_ref, mixed_ref, mt_ref, bands_ref, do_ref, dqa_ref, dka_ref, corr_ref, kx_ref):
    length = qkv_ref.shape[1]
    tiles = length // TILE
    scale = 1.0 / math.sqrt(DH)
    group = pl.program_id(0)

    @pl.when(jnp.logical_and(group == 0, pl.program_id(1) == 0))
    def _():
        d_ref[...] = jnp.zeros_like(d_ref)
        dlow_ref[...] = jnp.zeros_like(dlow_ref)
        mt_ref[...] = jnp.zeros_like(mt_ref)

    @pl.when(pl.program_id(1) == 0)
    def _():
        corr_ref[...] = jnp.zeros_like(corr_ref)
        gmix_ref[...] = jnp.zeros_like(gmix_ref)
        ggain_ref[...] = jnp.zeros_like(ggain_ref)

    gain_total = jnp.zeros((1, PAIR), f32)
    for tile in range(tiles):
        first = tile * TILE
        span = first + TILE
        centred, inverse, masks = norm_parts(heads_ref[0, first:span, :])
        unit = centred * inverse
        outer = dj_ref[0, first:span, :].astype(f32)
        gain_total = gain_total + jnp.sum(outer * unit, axis=0, keepdims=True)
        inner = outer * gain_ref[...]
        result = inner
        for mask in masks:
            mean = jnp.sum(inner * mask, axis=1, keepdims=True) / DH
            along = jnp.sum(inner * unit * mask, axis=1, keepdims=True) / DH
            result = result - mask * (mean + unit * along)
        do_ref[first:span, :] = (result * inverse).astype(bf16)
    ggain_ref[0] = ggain_ref[0] + gain_total

    sums = [[jnp.zeros((1, 1), f32) for _ in range(2)] for _ in range(2)]
    mix = [[mix_ref[(group * 2 + head) * 2 + other] for other in range(2)] for head in range(2)]
    for tile in range(tiles):
        first = tile * TILE
        span = first + TILE
        probs = [jnp.where(lax.broadcasted_iota(jnp.int32, (TILE, span), 1) <= lax.broadcasted_iota(jnp.int32, (TILE, span), 0) + first, p_ref[0, 0, head, first:span, :span], 0.0) for head in range(2)]
        grads = []
        for head in range(2):
            mixed = (mix[head][0] * probs[0] + mix[head][1] * probs[1]).astype(bf16)
            mixed_ref[head, first:span, :span] = mixed
            grads.append(nt(do_ref[first:span, :] * head_lanes(head).astype(bf16), qkv_ref[0, :span, 2 * PAIR :]))
        for other in range(2):
            row_sum = jnp.zeros((TILE, 1), f32)
            for head in range(2):
                along = jnp.sum(grads[head] * probs[other], axis=1, keepdims=True)
                sums[head][other] = sums[head][other] + jnp.sum(along, axis=0, keepdims=True)
                row_sum = row_sum + mix[head][other] * along
            outer = mix[0][other] * grads[0] + mix[1][other] * grads[1]
            d_ref[other, first + PAD : span + PAD, :span] = probs[other] * (outer - row_sum)
            dlow_ref[other, first + PAD : span + PAD, :span] = d_ref[other, first + PAD : span + PAD, :span].astype(bf16)
    lane = lax.broadcasted_iota(jnp.int32, (1, TILE), 1)
    spread = jnp.zeros((1, TILE), f32)
    for head in range(2):
        for other in range(2):
            spread = spread + jnp.where(lane == head * 2 + other, sums[head][other], 0.0)
    gmix_ref[0] = gmix_ref[0] + spread

    for tile in range(tiles):
        first = tile * TILE
        total = jnp.zeros((TILE, PAIR), f32)
        for head in range(2):
            total = total + tn(mixed_ref[head, first:, first : first + TILE], do_ref[first:, :] * head_lanes(head).astype(bf16))
        dqkv_ref[0, first : first + TILE, 2 * PAIR :] = total.astype(bf16)

    dqa_ref[...] = jnp.zeros_like(dqa_ref)
    dka_ref[...] = jnp.zeros_like(dka_ref)

    shift_keys(qkv_ref[0, :, PAIR : 2 * PAIR], kx_ref)

    def one_head(head, carry):
        base = (group * 2 + head) * (QT * KT)
        fill_bands(kern_ref, base, bands_ref, None, lambda row, col: row - TILE - col + (KT - 1))
        lanes = head_lanes(head).astype(bf16)
        query = qkv_ref[0, :, :PAIR] * lanes
        for tile in range(tiles + 1):
            start = max(0, tile - 1) * TILE
            scores = nt(kx_ref[tile * TILE : (tile + 1) * TILE, :], query[start:]) * scale
            key = lax.broadcasted_iota(jnp.int32, (TILE, length - start), 0) + (tile * TILE - REACH)
            pos = lax.broadcasted_iota(jnp.int32, (TILE, length - start), 1) + start
            valid = jnp.logical_and(key >= 0, key <= pos)
            mt_ref[tile * TILE : (tile + 1) * TILE, start:] = jnp.where(valid, scores, 0.0).astype(bf16)
        for tile in range(tiles):
            start = max(0, tile - 1) * TILE
            count = length - start
            source = d_ref[head, start + PAD :, tile * TILE : (tile + 1) * TILE]
            moved = [source[:count].astype(bf16)]
            for lag in range(1, QT):
                moved.append(pltpu.roll(source, source.shape[0] - lag, 0)[:count].astype(bf16))
            stacked = jnp.concatenate(moved, axis=1)
            corr_ref[head] = corr_ref[head] + nn(mt_ref[tile * TILE : (tile + 2) * TILE, start:], stacked)
        for tile in range(tiles + 1):
            first = tile * TILE
            if tile == 0:
                wide = nn(dlow_ref[head, first:, :TILE], bands_ref[TILE:, :])
            elif tile == tiles:
                wide = nn(dlow_ref[head, first:, first - TILE : first], bands_ref[:TILE, :])
            else:
                wide = nn(dlow_ref[head, first:, first - TILE : first + TILE], bands_ref[...])
            total = wide[:, :TILE]
            rows = wide.shape[0]
            for lag in range(1, QT):
                total = total + pltpu.roll(wide[:, lag * TILE : (lag + 1) * TILE], rows - lag, 0)
            begin = max(0, first - PAD)
            total = total[begin - (first - PAD) : rows - PAD]
            grad = jnp.where(valid_keys(begin, length - begin, first), total, 0.0).astype(bf16)
            dqa_ref[begin:, :] = dqa_ref[begin:, :] + nn(grad, kx_ref[first : first + TILE, :] * lanes)
            dka_ref[first : first + TILE, :] = dka_ref[first : first + TILE, :] + tn(grad, query[begin:])
        return carry

    lax.fori_loop(0, 2, one_head, 0)
    dqkv_ref[0, :, :PAIR] = (dqa_ref[...] * scale).astype(bf16)
    keys = dka_ref[...]
    dqkv_ref[0, :, PAIR : 2 * PAIR] = (pltpu.roll(keys, keys.shape[0] - REACH, 0)[:length] * scale).astype(bf16)

    @pl.when(pl.program_id(1) == pl.num_programs(1) - 1)
    def _():
        row = lax.broadcasted_iota(jnp.int32, (2 * TILE, QT * TILE), 0)
        col = lax.broadcasted_iota(jnp.int32, (2 * TILE, QT * TILE), 1) % TILE
        for head in range(2):
            corr = corr_ref[head]
            for key_lag in range(KT):
                gk_ref[0, head, key_lag : key_lag + 1, :] = jnp.sum(jnp.where(row - col == (KT - 1) - key_lag, corr, 0.0), axis=0, keepdims=True)
            gk_ref[0, head, KT:, :] = jnp.zeros((16 - KT, QT * TILE), f32)


def block_specs(length):
    smem = pl.BlockSpec(memory_space=pltpu.SMEM)
    one = pl.BlockSpec((1, length, PAIR), lambda g, s: (s, 0, g))
    three = pl.BlockSpec((1, length, 3 * PAIR), lambda g, s: (s, 0, g))
    gain = pl.BlockSpec((1, PAIR), lambda g, s: (0, g))
    prob = pl.BlockSpec((1, 1, 2, length, length), lambda g, s: (s, g, 0, 0, 0))
    return smem, one, three, gain, prob


def attend_fwd(kern, mix, qkv, gain):
    seqs, length, width = qkv.shape
    groups = width // (3 * PAIR)
    smem, one, three, gspec, prob = block_specs(length)
    rows = (seqs, length, groups * PAIR)
    return pl.pallas_call(
        attend_fwd_body,
        grid=(groups, seqs),
        in_specs=[smem, smem, three, gspec],
        out_specs=[one, one, prob],
        out_shape=[
            jax.ShapeDtypeStruct(rows, bf16),
            jax.ShapeDtypeStruct(rows, f32),
            jax.ShapeDtypeStruct((seqs, groups, 2, length, length), f32),
        ],
        scratch_shapes=[
            pltpu.VMEM((length + PAD, length + TILE), bf16),
            pltpu.VMEM((length + PAD, length + TILE), bf16),
            pltpu.VMEM((2 * TILE, QT * TILE), bf16),
            pltpu.VMEM((2 * TILE, QT * TILE), bf16),
            pltpu.VMEM((length + TILE, PAIR), bf16),
        ],
        name="attend_fwd",
    )(kern, mix, qkv, gain)


def attend_bwd(kern, mix, qkv, gain, heads, probs, outer):
    seqs, length, width = qkv.shape
    groups = width // (3 * PAIR)
    smem, one, three, gspec, prob = block_specs(length)
    return pl.pallas_call(
        attend_bwd_body,
        grid=(groups, seqs),
        in_specs=[smem, smem, three, gspec, one, prob, one],
        out_specs=[
            three,
            pl.BlockSpec((1, 2, 16, QT * TILE), lambda g, s: (g, 0, 0, 0)),
            pl.BlockSpec((1, 1, TILE), lambda g, s: (g, 0, 0)),
            pl.BlockSpec((1, 1, PAIR), lambda g, s: (g, 0, 0)),
        ],
        out_shape=[
            jax.ShapeDtypeStruct(qkv.shape, bf16),
            jax.ShapeDtypeStruct((groups, 2, 16, QT * TILE), f32),
            jax.ShapeDtypeStruct((groups, 1, TILE), f32),
            jax.ShapeDtypeStruct((groups, 1, PAIR), f32),
        ],
        scratch_shapes=[
            pltpu.VMEM((2, length + 2 * PAD, length), f32),
            pltpu.VMEM((2, length + 2 * PAD, length), bf16),
            pltpu.VMEM((2, length, length), bf16),
            pltpu.VMEM((length + TILE, length), bf16),
            pltpu.VMEM((2 * TILE, QT * TILE), bf16),
            pltpu.VMEM((length, PAIR), bf16),
            pltpu.VMEM((length, PAIR), f32),
            pltpu.VMEM((length + TILE, PAIR), f32),
            pltpu.VMEM((2, 2 * TILE, QT * TILE), f32),
            pltpu.VMEM((length + TILE, PAIR), bf16),
        ],
        name="attend_bwd",
    )(kern, mix, qkv, gain, heads, probs, outer)


def xor_perm(count, bit):
    return [(index, index ^ bit) for index in range(count)]


def swap(value, axis, bit):
    return lax.ppermute(value, axis, xor_perm(lax.axis_size(axis), bit))


def place(pieces, count, here):
    rows, cols = pieces[0].shape
    out = jnp.zeros((count * rows, cols), pieces[0].dtype)
    for offset, piece in pieces.items():
        out = lax.dynamic_update_slice(out, piece, ((here ^ offset) * rows, 0))
    return out


def far_bits(count):
    bits = []
    bit = 2
    while bit < count:
        bits.append(bit)
        bit *= 2
    return bits


def batch_gather(value):
    count = lax.axis_size("batch")
    here = lax.axis_index("batch")
    bits = far_bits(count)
    pieces = {0: value}
    if len(bits) == 2:
        half = value.shape[0] // 2
        one, two = bits
        pieces[one] = swap(value, "batch", one)
        pieces[two] = swap(value, "batch", two)
        upper = swap(pieces[one][:half], "batch", two)
        lower = swap(pieces[two][half:], "batch", one)
        near = {offset: swap(piece, "batch", 1) for offset, piece in pieces.items()}
        near_upper = swap(upper, "batch", 1)
        near_lower = swap(lower, "batch", 1)
        rows, cols = value.shape
        out = jnp.zeros((count * rows, cols), value.dtype)
        for offset, piece in pieces.items():
            out = lax.dynamic_update_slice(out, piece, ((here ^ offset) * rows, 0))
            out = lax.dynamic_update_slice(out, near[offset], ((here ^ offset ^ 1) * rows, 0))
        both = one ^ two
        out = lax.dynamic_update_slice(out, upper, ((here ^ both) * rows, 0))
        out = lax.dynamic_update_slice(out, lower, ((here ^ both) * rows + half, 0))
        out = lax.dynamic_update_slice(out, near_upper, ((here ^ both ^ 1) * rows, 0))
        out = lax.dynamic_update_slice(out, near_lower, ((here ^ both ^ 1) * rows + half, 0))
        return out
    for bit in bits + [1]:
        pieces.update({offset ^ bit: swap(piece, "batch", bit) for offset, piece in pieces.items()})
    return place(pieces, count, here)


def batch_scatter(value):
    count = lax.axis_size("batch")
    here = lax.axis_index("batch")
    bits = far_bits(count)
    rows = value.shape[0] // count

    def block(offset):
        return lax.dynamic_slice_in_dim(value, (here ^ offset) * rows, rows, 0)

    def add(left, right):
        return left.astype(f32) + right.astype(f32)

    offsets = [0]
    for bit in bits:
        offsets = offsets + [offset ^ bit for offset in offsets]
    came = {offset: swap(block(offset ^ 1), "batch", 1) for offset in reversed(offsets)}
    sums = {offset: add(block(offset), came[offset]) for offset in offsets}
    if len(bits) == 2:
        one, two = bits
        half = rows // 2
        far = sums[one ^ two].astype(bf16)
        upper = swap(far[:half], "batch", one)
        lower = swap(far[half:], "batch", two)
        via_two = jnp.concatenate([add(sums[two][:half], upper), sums[two][half:]], axis=0)
        via_one = jnp.concatenate([sums[one][:half], add(sums[one][half:], lower)], axis=0)
        from_one = swap(via_one.astype(bf16), "batch", one)
        from_two = swap(via_two.astype(bf16), "batch", two)
        return sums[0] + from_one.astype(f32) + from_two.astype(f32)
    for bit in reversed(bits):
        offsets = [offset for offset in offsets if not offset & bit]
        sums = {
            offset: add(sums[offset], swap(sums[offset ^ bit].astype(bf16), "batch", bit))
            for offset in offsets
        }
    return sums[0]


def line_perms(count):
    up = [(index, index + 1) for index in range(count - 1)]
    down = [(index + 1, index) for index in range(count - 1)]
    return up, down


def seq_gather(value):
    count = lax.axis_size("seq")
    here = lax.axis_index("seq")
    up, down = line_perms(count)
    rows = value.shape[0]
    rising, falling = [value], [value]
    for _ in range(count - 1):
        rising.append(lax.ppermute(rising[-1], "seq", up))
        falling.append(lax.ppermute(falling[-1], "seq", down))
    out = jnp.zeros((count * rows, value.shape[1]), value.dtype)
    out = lax.dynamic_update_slice(out, value, (here * rows, 0))
    for step in range(1, count):
        piece = jnp.where(here >= step, rising[step], falling[count - step])
        out = lax.dynamic_update_slice(out, piece, (((here - step) % count) * rows, 0))
    return out


def seq_scatter(value):
    count = lax.axis_size("seq")
    here = lax.axis_index("seq")
    up, down = line_perms(count)
    rows = value.shape[0] // count

    def block(index):
        return lax.dynamic_slice_in_dim(value, jnp.clip(index, 0, count - 1) * rows, rows, 0)

    rising = falling = None
    for step in range(1, count):
        far = count - step
        top, low = block(here + far), block(here - far)
        if rising is not None:
            top = (top.astype(f32) + rising.astype(f32)).astype(bf16)
            low = (low.astype(f32) + falling.astype(f32)).astype(bf16)
        rising = lax.ppermute(top, "seq", up)
        falling = lax.ppermute(low, "seq", down)
    return block(here).astype(f32) + rising.astype(f32) + falling.astype(f32)


def seq_swap(blocks):
    count = lax.axis_size("seq")
    here = lax.axis_index("seq")
    out = jnp.zeros_like(blocks)
    own = lax.dynamic_index_in_dim(blocks, here, 0, True)
    out = lax.dynamic_update_slice_in_dim(out, own, here, 0)
    for step in range(1, count):
        piece = lax.dynamic_index_in_dim(blocks, (here + step) % count, 0, True)
        perm = [(index, (index + step) % count) for index in range(count)]
        piece = lax.ppermute(piece, "seq", perm)
        out = lax.dynamic_update_slice_in_dim(out, piece, (here - step) % count, 0)
    return out


def all_sum(value):
    for axis in ("batch", "seq"):
        bit = 1
        while bit < lax.axis_size(axis):
            value = value + swap(value, axis, bit)
            bit *= 2
    return value


def pad_pairs(value):
    lead = value.shape[0]
    pairs = value.reshape(lead, -1, 2 * DH)
    return jnp.pad(pairs, ((0, 0), (0, 0), (0, PAIR - 2 * DH))).reshape(lead, -1)


def cut_pairs(value):
    lead = value.shape[0]
    return value.reshape(lead, -1, PAIR)[:, :, : 2 * DH].reshape(lead, -1)


def inverse_rms(values):
    return lax.rsqrt(jnp.mean(values * values, axis=-1, keepdims=True) + 1e-06)


def rms_back(values, inverse, inner):
    along = jnp.mean(values * inner, axis=-1, keepdims=True)
    return inverse * (inner - values * (inverse * inverse) * along)


def per_device(
    inputs,
    output_grad,
    source_tags,
    source_counts,
    gain_in,
    w_query,
    w_key,
    w_value,
    kernel,
    mixing,
    gain_head,
    w_out,
    gain_mid,
    w_gate,
    w_up,
    w_down,
):
    seqs, seg, width = inputs.shape
    parts = lax.axis_size("seq")
    lanes = lax.axis_size("batch")
    place_seq = lax.axis_index("seq")
    place_batch = lax.axis_index("batch")
    length = seg * parts
    groups = H // (2 * parts)
    local = groups * 2 * DH
    own = w_query.shape[0]
    blocks = parts * lanes

    joint = jnp.stack([w_query, w_key, w_value], axis=1).reshape(own, 3, parts, groups, 2 * DH)
    joint = joint.transpose(2, 0, 3, 1, 4).reshape(parts, own, 3 * local)
    gains = jnp.stack([gain_in, gain_head, gain_mid]).reshape(1, 1, 3 * own)
    gains = jnp.pad(gains, ((0, 0), (0, 15), (0, 3 * local - 3 * own)))
    packed = jnp.concatenate([joint, jnp.broadcast_to(gains, (parts, 16, 3 * local))], axis=1)
    packed = seq_swap(packed)
    order = [
        (index, (index % lanes) * parts + index // lanes) for index in range(blocks)
    ]
    out_rows = lax.ppermute(w_out, ("batch", "seq"), order)
    flat_rows = own * width // (3 * local)
    gain_row = packed[:, own, : 3 * own].reshape(1, parts * 3 * own)
    gain_row = jnp.pad(gain_row, ((0, 15), (0, 3 * local - parts * 3 * own)))
    shard = jnp.concatenate(
        [packed[:, :own].reshape(parts * own, 3 * local), gain_row, out_rows.reshape(flat_rows, 3 * local)],
        axis=0,
    )
    gathered = batch_gather(shard).reshape(lanes, -1, 3 * local)
    w_joint = pad_pairs(gathered[:, : parts * own].reshape(width, 3 * local))
    gain_rows = gathered[:, parts * own, : parts * 3 * own].reshape(lanes, parts, 3, own)
    all_gains = gain_rows.transpose(2, 0, 1, 3).reshape(3, 1, width).astype(f32)
    gain_in32, gain_head32, gain_mid32 = all_gains[0], all_gains[1], all_gains[2]
    gain_own = pad_pairs(lax.dynamic_slice_in_dim(gain_head32, place_seq * local, local, 1))
    w_join = gathered[:, parts * own + 16 :].reshape(local, width)
    w_join = jnp.pad(
        w_join.reshape(groups, 2 * DH, width), ((0, 0), (0, PAIR - 2 * DH), (0, 0))
    ).reshape(groups * PAIR, width)
    kern_own = lax.dynamic_slice_in_dim(
        kernel.reshape(-1), place_seq * (2 * groups * QT * KT), 2 * groups * QT * KT, 0
    )
    mix_own = lax.dynamic_slice_in_dim(mixing.reshape(-1), place_seq * 4 * groups, 4 * groups, 0)

    x_all = [seq_gather(inputs[index]) for index in range(seqs)]
    w_gate_up = batch_gather(jnp.concatenate([w_gate, w_up], axis=1))
    w_down_t = batch_gather(w_down.T)
    hidden_width = w_gate.shape[1]
    o_all = [seq_gather(output_grad[index]) for index in range(seqs)]

    source_ids = jnp.arange(source_counts.shape[0], dtype=jnp.int32)
    tag_count = jnp.sum(
        jnp.where(source_tags[:, None] == source_ids[None, :], source_counts[None, :], 0), axis=1
    )
    factor = length / tag_count.astype(f32)

    outputs, input_grads = [], []
    keep = []
    for index in range(seqs):
        x32 = x_all[index].astype(f32)
        x_inverse = inverse_rms(x32)
        normed = (x32 * x_inverse * gain_in32).astype(bf16)
        qkv = nn(normed, w_joint).astype(bf16)[None]
        joined, heads, probs = attend_fwd(kern_own, mix_own, qkv, gain_own)
        middle = inputs[index].astype(f32) + seq_scatter(nn(joined[0], w_join).astype(bf16))
        keep.append([x_inverse, normed, qkv, joined, heads, probs, middle])
    gain_mid_grad = jnp.zeros((1, width), f32)
    gain_in_grad = jnp.zeros((1, width), f32)
    ffn = []
    for index in range(seqs):
        middle = keep[index][-1]
        mid_inverse = inverse_rms(middle)
        n_all = seq_gather((middle * mid_inverse * gain_mid32).astype(bf16))
        both = nn(n_all, w_gate_up)
        gate, upward = both[:, :hidden_width], both[:, hidden_width:]
        sigma = 1.0 / (1.0 + jnp.exp(-gate))
        silu = gate * sigma
        hidden = (silu * upward).astype(bf16)
        down_in = (o_all[index].astype(f32) * factor[index]).astype(bf16)
        hidden_grad = nn(down_in, w_down_t)
        gate_grad = (hidden_grad * upward * (sigma * (1.0 + gate * (1.0 - sigma)))).astype(bf16)
        up_grad = (hidden_grad * silu).astype(bf16)
        grads = jnp.concatenate([gate_grad, up_grad], axis=1)
        mid_grad = seq_scatter(nt(grads, w_gate_up).astype(bf16))
        result = middle + seq_scatter(nt(hidden, w_down_t).astype(bf16))
        outputs.append(result.astype(bf16))
        ffn.append((n_all, hidden, down_in, grads))
        unit = middle * mid_inverse
        gain_mid_grad = gain_mid_grad + jnp.sum(mid_grad * unit, axis=0, keepdims=True)
        cotangent = output_grad[index].astype(f32) * factor[index]
        middle_grad = cotangent + rms_back(middle, mid_inverse, mid_grad * gain_mid32)
        a_all = seq_gather(middle_grad.astype(bf16))
        keep[index] += [middle_grad, a_all]
    cat = lambda place: jnp.concatenate([item[place] for item in ffn], axis=0)
    all_n, all_hidden, all_down, all_grads = cat(0), cat(1), cat(2), cat(3)
    g_gate_up = batch_scatter(tn(all_n, all_grads).astype(bf16))
    g_down_t = batch_scatter(tn(all_down, all_hidden).astype(bf16))
    back = []
    for index in range(seqs):
        x_inverse, normed, qkv, joined, heads, probs, middle, middle_grad, a_all = keep[index]
        outer = nt(a_all, w_join)[None]
        dqkv, corr, mix_sum, head_sum = attend_bwd(
            kern_own, mix_own, qkv, gain_own, heads, probs, outer
        )
        n_part = nt(dqkv[0], w_joint)
        unit_all = x_all[index].astype(f32) * x_inverse
        gain_in_grad = gain_in_grad + jnp.sum(n_part * unit_all, axis=0, keepdims=True)
        n_grad = seq_scatter(n_part.astype(bf16))
        x32 = inputs[index].astype(f32)
        inner = rms_back(x32, inverse_rms(x32), n_grad * gain_in32)
        input_grads.append((middle_grad + inner).astype(bf16))
        back.append((normed, dqkv[0], joined[0], a_all, corr, mix_sum, head_sum))
    cat = lambda place: jnp.concatenate([item[place] for item in back], axis=0)
    all_normed, all_dqkv, all_joined, all_a = cat(0), cat(1), cat(2), cat(3)
    g_out = tn(all_joined, all_a).astype(bf16)
    g_out = g_out.reshape(groups, PAIR, width)[:, : 2 * DH].reshape(local, width)
    g_out = batch_scatter(g_out)
    g_out = lax.ppermute(g_out, ("batch", "seq"), [(there, here) for here, there in order])
    g_joint = batch_scatter(cut_pairs(tn(all_normed, all_dqkv)).astype(bf16))
    g_joint = seq_swap(g_joint.astype(bf16).reshape(parts, own, 3 * local)).astype(f32)
    g_joint = g_joint.reshape(parts, own, groups, 3, 2 * DH).transpose(3, 1, 0, 2, 4)
    g_joint = g_joint.reshape(3, own, width)

    corr = sum(item[4] for item in back)
    mix_sum = sum(item[5] for item in back)
    head_sum = sum(item[6] for item in back)
    kern_grad = corr[:, :, :KT].reshape(2 * groups, KT, QT, TILE).sum(-1).transpose(0, 2, 1)
    mix_grad = mix_sum[:, 0, :4].reshape(-1)
    head_grad = head_sum[:, 0, : 2 * DH].reshape(-1)

    def spread(value, total):
        return lax.dynamic_update_slice_in_dim(
            jnp.zeros((total,), f32), value.reshape(-1), place_seq * value.size, 0
        )

    small = jnp.concatenate(
        [
            gain_in_grad[0],
            gain_mid_grad[0],
            spread(head_grad, width),
            spread(kern_grad, H * QT * KT),
            spread(mix_grad, H * 2),
        ]
    )
    size = small.size
    small = jnp.pad(small, (0, -size % 1024)).reshape(-1, 128)
    small = all_sum(small).reshape(-1)
    start = (place_batch * parts + place_seq) * own
    cuts = [lax.dynamic_slice_in_dim(small, start + step * width, own, 0) for step in range(3)]
    kernel_sum = small[3 * width : 3 * width + H * QT * KT].reshape(kernel.shape)
    mixing_sum = small[3 * width + H * QT * KT : size].reshape(mixing.shape)
    return (
        jnp.stack(outputs),
        jnp.stack(input_grads),
        cuts[0],
        g_joint[0],
        g_joint[1],
        g_joint[2],
        kernel_sum,
        mixing_sum,
        cuts[2],
        g_out,
        cuts[1],
        g_gate_up[:, :hidden_width],
        g_gate_up[:, hidden_width:],
        g_down_t.T,
    )


def solution(mesh):
    rows = P(("batch", "seq"))
    mats = P(("batch", "seq"), None)
    tokens = P("batch", "seq", None)
    in_specs = (
        tokens,
        tokens,
        P("batch"),
        P(),
        rows,
        mats,
        mats,
        mats,
        P(),
        P(),
        rows,
        mats,
        rows,
        P("batch", "seq"),
        P("batch", "seq"),
        P("seq", "batch"),
    )
    out_specs = (
        tokens,
        tokens,
        rows,
        mats,
        mats,
        mats,
        P(),
        P(),
        rows,
        mats,
        rows,
        P("batch", "seq"),
        P("batch", "seq"),
        P("seq", "batch"),
    )
    return jax.shard_map(
        per_device, mesh=mesh, in_specs=in_specs, out_specs=out_specs, check_vma=False
    )
```

```python
import math

import jax
import jax.numpy as jnp
from jax import lax
from jax.experimental import pallas as pl
from jax.experimental.pallas import tpu as pltpu
from jax.sharding import PartitionSpec as P

H = 16
DH = 96
QUERY_TAPS = 6
KEY_TAPS = 11
REACH = KEY_TAPS // 2
TILE = 128
PAD = 16
bf16 = jnp.bfloat16
f32 = jnp.float32


def nn(left, right):
    return lax.dot_general(left, right, (((1,), (0,)), ((), ())), preferred_element_type=f32)


def nt(left, right):
    return lax.dot_general(left, right, (((1,), (1,)), ((), ())), preferred_element_type=f32)


def tn(left, right):
    return lax.dot_general(left, right, (((0,), (0,)), ((), ())), preferred_element_type=f32)


def lanes_of(begin, width):
    lane = lax.broadcasted_iota(jnp.int32, (1, width), 1)
    return jnp.logical_and(lane >= begin, lane < begin + DH).astype(f32)


def split(value):
    high = value.astype(bf16)
    return high, (value - high.astype(f32)).astype(bf16)


def fill_bands(kern_ref, base, bands, low_bands, offset):
    row = lax.broadcasted_iota(jnp.int32, (2 * TILE, TILE), 0)
    col = lax.broadcasted_iota(jnp.int32, (2 * TILE, TILE), 1)
    tap = offset(row, col)
    for lag in range(QUERY_TAPS):
        band = jnp.zeros((2 * TILE, TILE), f32)
        for key_lag in range(KEY_TAPS):
            band = jnp.where(tap == key_lag, kern_ref[base + lag * KEY_TAPS + key_lag], band)
        high, low = split(band)
        bands[:, lag * TILE : (lag + 1) * TILE] = high
        if low_bands is not None:
            low_bands[:, lag * TILE : (lag + 1) * TILE] = low


def valid_keys(first_query, rows, first_key):
    query = lax.broadcasted_iota(jnp.int32, (rows, TILE), 0) + first_query
    key = lax.broadcasted_iota(jnp.int32, (rows, TILE), 1) + (first_key - REACH)
    return jnp.logical_and(key >= 0, key <= query)


def shift_keys(keys, kx_ref):
    tail = jnp.zeros((TILE, keys.shape[1]), f32)
    moved = jnp.concatenate([keys.astype(f32), tail], axis=0)
    kx_ref[...] = pltpu.roll(moved, REACH, 0).astype(bf16)


def norm_parts(heads):
    masks = [lanes_of(head * DH, heads.shape[1]) for head in range(heads.shape[1] // DH)]
    means = jnp.zeros_like(heads)
    for mask in masks:
        means = means + mask * (jnp.sum(heads * mask, axis=1, keepdims=True) / DH)
    centred = heads - means
    inverse = jnp.zeros_like(heads)
    for mask in masks:
        spread = jnp.sum(centred * centred * mask, axis=1, keepdims=True) / DH
        inverse = inverse + mask * lax.rsqrt(spread + 1e-05)
    return centred, inverse, masks


def pair_slice(pair, local, part):
    span = min(2 * TILE, local)
    start = (3 * pair) // 2 * TILE
    if not isinstance(pair, int):
        start = pl.multiple_of(start, TILE)
    return pl.ds(part * local + start, span), pair * 2 * DH - start


def attend_fwd_body(
    kern_ref, mix_ref, qkv_ref, gain_ref,
    joined_ref, heads_ref, p_ref,
    high_ref, low_ref, bands_ref, low_bands_ref, kx_ref,
):
    length = qkv_ref.shape[1]
    local = heads_ref.shape[2]
    span_pair = kx_ref.shape[1]
    tiles = length // TILE
    pairs = local // (2 * DH)
    scale = 1.0 / math.sqrt(DH)

    @pl.when(pl.program_id(0) == 0)
    def _():
        high_ref[...] = jnp.zeros_like(high_ref)
        low_ref[...] = jnp.zeros_like(low_ref)

    heads_ref[...] = jnp.zeros_like(heads_ref)

    def one_pair(pair, carry):
        q_at, offset = pair_slice(pair, local, 0)
        k_at, _ = pair_slice(pair, local, 1)
        v_at, _ = pair_slice(pair, local, 2)
        h_at, _ = pair_slice(pair, local, 0)
        shift_keys(qkv_ref[0, :, k_at], kx_ref)

        def one_head(head, inner):
            base = (pair * 2 + head) * (QUERY_TAPS * KEY_TAPS)
            fill_bands(
                kern_ref, base, bands_ref, low_bands_ref, lambda row, col: (KEY_TAPS - 1) - (row - col)
            )
            query = qkv_ref[0, :, q_at] * lanes_of(offset + head * DH, span_pair).astype(bf16)
            for tile in range(tiles + 1):
                at = slice(tile * TILE, (tile + 1) * TILE)
                first = max(0, tile * TILE - PAD)
                scores = nt(query[first:], kx_ref[at, :]) * scale
                masked = jnp.where(valid_keys(first, length - first, tile * TILE), scores, 0.0)
                high, low = split(masked)
                high_ref[first + PAD :, at] = high
                low_ref[first + PAD :, at] = low
            for tile in range(tiles):
                first = tile * TILE
                high = high_ref[first:, first : first + 2 * TILE]
                low = low_ref[first:, first : first + 2 * TILE]
                bands = bands_ref[...]
                wide = nn(high, bands) + nn(low, bands) + nn(high, low_bands_ref[...])
                total = wide[:, :TILE]
                for lag in range(1, QUERY_TAPS):
                    total = total + pltpu.roll(wide[:, lag * TILE : (lag + 1) * TILE], lag, 0)
                p_ref[0, pair, head, first:, first : first + TILE] = total[PAD:]
            return inner

        lax.fori_loop(0, 2, one_head, 0)
        for tile in range(tiles):
            first = tile * TILE
            span = first + TILE
            query = lax.broadcasted_iota(jnp.int32, (TILE, span), 0) + first
            key = lax.broadcasted_iota(jnp.int32, (TILE, span), 1)
            valid = key <= query
            probs = []
            for head in range(2):
                logits = jnp.where(valid, p_ref[0, pair, head, first:span, :span], -1e30)
                top = jnp.max(logits, axis=1, keepdims=True)
                expon = jnp.where(valid, jnp.exp(logits - top), 0.0)
                prob = expon / jnp.sum(expon, axis=1, keepdims=True)
                p_ref[0, pair, head, first:span, :span] = prob
                probs.append(prob)
            out = heads_ref[0, first:span, h_at]
            for head in range(2):
                spot = (pair * 2 + head) * 2
                mixed = (mix_ref[spot] * probs[0] + mix_ref[spot + 1] * probs[1]).astype(bf16)
                mask = lanes_of(offset + head * DH, span_pair).astype(bf16)
                out = out + nn(mixed, qkv_ref[0, :span, v_at] * mask)
            heads_ref[0, first:span, h_at] = out
        return carry

    if pairs == 1:
        one_pair(0, 0)
    else:
        lax.fori_loop(0, pairs, one_pair, 0)
    for tile in range(tiles):
        at = slice(tile * TILE, (tile + 1) * TILE)
        centred, inverse, _ = norm_parts(heads_ref[0, at, :])
        joined_ref[0, at, :] = (centred * inverse * gain_ref[...]).astype(bf16)


def attend_bwd_body(
    kern_ref, mix_ref, qkv_ref, gain_ref, heads_ref, p_ref, dj_ref,
    dqkv_ref, gk_ref, gmix_ref, ggain_ref,
    d_ref, dlow_ref, mixed_ref, mt_ref, bands_ref, do_ref, acc_ref, corr_ref, kx_ref, dka_ref,
):
    length = qkv_ref.shape[1]
    local = heads_ref.shape[2]
    span_pair = kx_ref.shape[1]
    tiles = length // TILE
    pairs = local // (2 * DH)
    scale = 1.0 / math.sqrt(DH)
    lane = lax.broadcasted_iota(jnp.int32, (1, TILE), 1)

    @pl.when(pl.program_id(0) == 0)
    def _():
        d_ref[...] = jnp.zeros_like(d_ref)
        dlow_ref[...] = jnp.zeros_like(dlow_ref)
        mt_ref[...] = jnp.zeros_like(mt_ref)
        corr_ref[...] = jnp.zeros_like(corr_ref)
        gmix_ref[...] = jnp.zeros_like(gmix_ref)
        ggain_ref[...] = jnp.zeros_like(ggain_ref)

    gain_total = jnp.zeros((1, local), f32)
    for tile in range(tiles):
        at = slice(tile * TILE, (tile + 1) * TILE)
        centred, inverse, masks = norm_parts(heads_ref[0, at, :])
        unit = centred * inverse
        outer = dj_ref[0, at, :].astype(f32)
        gain_total = gain_total + jnp.sum(outer * unit, axis=0, keepdims=True)
        inner = outer * gain_ref[...]
        result = inner
        for mask in masks:
            mean = jnp.sum(inner * mask, axis=1, keepdims=True) / DH
            along = jnp.sum(inner * unit * mask, axis=1, keepdims=True) / DH
            result = result - mask * (mean + unit * along)
        do_ref[at, :] = (result * inverse).astype(bf16)
    ggain_ref[...] = ggain_ref[...] + gain_total
    acc_ref[...] = jnp.zeros_like(acc_ref)

    def one_pair(pair, carry):
        q_at, offset = pair_slice(pair, local, 0)
        k_at, _ = pair_slice(pair, local, 1)
        v_at, _ = pair_slice(pair, local, 2)
        h_at, _ = pair_slice(pair, local, 0)
        shift_keys(qkv_ref[0, :, k_at], kx_ref)
        dka_ref[...] = jnp.zeros_like(dka_ref)
        sums = [[jnp.zeros((1, 1), f32) for _ in range(2)] for _ in range(2)]
        mix = [[mix_ref[(pair * 2 + head) * 2 + other] for other in range(2)] for head in range(2)]
        head_masks = [lanes_of(offset + head * DH, span_pair).astype(bf16) for head in range(2)]
        for tile in range(tiles):
            first = tile * TILE
            span = first + TILE
            query = lax.broadcasted_iota(jnp.int32, (TILE, span), 0) + first
            valid = lax.broadcasted_iota(jnp.int32, (TILE, span), 1) <= query
            probs = [
                jnp.where(valid, p_ref[0, pair, head, first:span, :span], 0.0) for head in range(2)
            ]
            grads = []
            for head in range(2):
                mixed = (mix[head][0] * probs[0] + mix[head][1] * probs[1]).astype(bf16)
                mixed_ref[head, first:span, :span] = mixed
                grads.append(nt(do_ref[first:span, h_at] * head_masks[head], qkv_ref[0, :span, v_at]))
            for other in range(2):
                row_sum = jnp.zeros((TILE, 1), f32)
                for head in range(2):
                    along = jnp.sum(grads[head] * probs[other], axis=1, keepdims=True)
                    sums[head][other] = sums[head][other] + jnp.sum(along, axis=0, keepdims=True)
                    row_sum = row_sum + mix[head][other] * along
                outer = mix[0][other] * grads[0] + mix[1][other] * grads[1]
                inner = probs[other] * (outer - row_sum)
                d_ref[other, first + PAD : span + PAD, :span] = inner
                dlow_ref[other, first + PAD : span + PAD, :span] = inner.astype(bf16)
        spread = jnp.zeros((1, TILE), f32)
        for head in range(2):
            for other in range(2):
                spread = spread + jnp.where(
                    lane == pair * 4 + head * 2 + other, sums[head][other], 0.0
                )
        gmix_ref[...] = gmix_ref[...] + spread

        for tile in range(tiles):
            first = tile * TILE
            at = slice(first, first + TILE)
            total = acc_ref[at, v_at]
            for head in range(2):
                total = total + tn(mixed_ref[head, first:, at], do_ref[first:, h_at] * head_masks[head])
            acc_ref[at, v_at] = total

        def one_head(head, inner):
            base = (pair * 2 + head) * (QUERY_TAPS * KEY_TAPS)
            fill_bands(
                kern_ref, base, bands_ref, None, lambda row, col: row - TILE - col + (KEY_TAPS - 1)
            )
            lanes = lanes_of(offset + head * DH, span_pair).astype(bf16)
            query = qkv_ref[0, :, q_at] * lanes
            for tile in range(tiles + 1):
                start = max(0, tile - 1) * TILE
                at = slice(tile * TILE, (tile + 1) * TILE)
                scores = nt(kx_ref[at, :], query[start:]) * scale
                key = lax.broadcasted_iota(jnp.int32, (TILE, length - start), 0) + (tile * TILE - REACH)
                pos = lax.broadcasted_iota(jnp.int32, (TILE, length - start), 1) + start
                valid = jnp.logical_and(key >= 0, key <= pos)
                mt_ref[at, start:] = jnp.where(valid, scores, 0.0).astype(bf16)
            total_corr = corr_ref[pair * 2 + head]
            for tile in range(tiles):
                start = max(0, tile - 1) * TILE
                count = length - start
                source = d_ref[head, start + PAD :, tile * TILE : (tile + 1) * TILE]
                moved = [source[:count].astype(bf16)]
                for lag in range(1, QUERY_TAPS):
                    moved.append(pltpu.roll(source, source.shape[0] - lag, 0)[:count].astype(bf16))
                stacked = jnp.concatenate(moved, axis=1)
                total_corr = total_corr + nn(mt_ref[tile * TILE : (tile + 2) * TILE, start:], stacked)
            corr_ref[pair * 2 + head] = total_corr
            for tile in range(tiles + 1):
                first = tile * TILE
                at = slice(first, first + TILE)
                if tile == 0:
                    wide = nn(dlow_ref[head, first:, :TILE], bands_ref[TILE:, :])
                elif tile == tiles:
                    wide = nn(dlow_ref[head, first:, first - TILE : first], bands_ref[:TILE, :])
                else:
                    wide = nn(dlow_ref[head, first:, first - TILE : first + TILE], bands_ref[...])
                total = wide[:, :TILE]
                rows = wide.shape[0]
                for lag in range(1, QUERY_TAPS):
                    total = total + pltpu.roll(wide[:, lag * TILE : (lag + 1) * TILE], rows - lag, 0)
                begin = max(0, first - PAD)
                total = total[begin - (first - PAD) : rows - PAD]
                grad = jnp.where(valid_keys(begin, length - begin, first), total, 0.0).astype(bf16)
                acc_ref[begin:, q_at] = acc_ref[begin:, q_at] + nn(grad, kx_ref[at, :] * lanes) * scale
                dka_ref[at, :] = dka_ref[at, :] + tn(grad, query[begin:])
            return inner

        lax.fori_loop(0, 2, one_head, 0)
        keys = dka_ref[...]
        back = pltpu.roll(keys, keys.shape[0] - REACH, 0)[:length] * scale
        acc_ref[:, k_at] = acc_ref[:, k_at] + back
        return carry

    if pairs == 1:
        one_pair(0, 0)
    else:
        lax.fori_loop(0, pairs, one_pair, 0)
    dqkv_ref[0] = acc_ref[...].astype(bf16)

    @pl.when(pl.program_id(0) == pl.num_programs(0) - 1)
    def _():
        row = lax.broadcasted_iota(jnp.int32, (2 * TILE, QUERY_TAPS * TILE), 0)
        col = lax.broadcasted_iota(jnp.int32, (2 * TILE, QUERY_TAPS * TILE), 1) % TILE

        def one_head(head, carry):
            corr = corr_ref[head]
            taps = [
                jnp.sum(jnp.where(row - col == (KEY_TAPS - 1) - key_lag, corr, 0.0), axis=0, keepdims=True)
                for key_lag in range(KEY_TAPS)
            ]
            taps.append(jnp.zeros((16 - KEY_TAPS, QUERY_TAPS * TILE), f32))
            gk_ref[head] = jnp.concatenate(taps, axis=0)
            return carry

        lax.fori_loop(0, 2 * pairs, one_head, 0)


def attend_fwd(kern, mix, qkv, gain):
    seqs, length, width = qkv.shape
    local = width // 3
    pairs = local // (2 * DH)
    smem = pl.BlockSpec(memory_space=pltpu.SMEM)
    one = pl.BlockSpec((1, length, local), lambda s: (s, 0, 0))
    return pl.pallas_call(
        attend_fwd_body,
        grid=(seqs,),
        in_specs=[
            smem,
            smem,
            pl.BlockSpec((1, length, width), lambda s: (s, 0, 0)),
            pl.BlockSpec((1, local), lambda s: (0, 0)),
        ],
        out_specs=[one, one, pl.BlockSpec((1, pairs, 2, length, length), lambda s: (s, 0, 0, 0, 0))],
        out_shape=[
            jax.ShapeDtypeStruct((seqs, length, local), bf16),
            jax.ShapeDtypeStruct((seqs, length, local), f32),
            jax.ShapeDtypeStruct((seqs, pairs, 2, length, length), f32),
        ],
        scratch_shapes=[
            pltpu.VMEM((length + PAD, length + TILE), bf16),
            pltpu.VMEM((length + PAD, length + TILE), bf16),
            pltpu.VMEM((2 * TILE, QUERY_TAPS * TILE), bf16),
            pltpu.VMEM((2 * TILE, QUERY_TAPS * TILE), bf16),
            pltpu.VMEM((length + TILE, min(2 * TILE, local)), bf16),
        ],
        name="attend_fwd",
    )(kern, mix, qkv, gain)


def attend_bwd(kern, mix, qkv, gain, heads, probs, outer):
    seqs, length, width = qkv.shape
    local = width // 3
    pairs = local // (2 * DH)
    span_pair = min(2 * TILE, local)
    smem = pl.BlockSpec(memory_space=pltpu.SMEM)
    one = pl.BlockSpec((1, length, local), lambda s: (s, 0, 0))
    wide = pl.BlockSpec((1, length, width), lambda s: (s, 0, 0))
    return pl.pallas_call(
        attend_bwd_body,
        grid=(seqs,),
        in_specs=[
            smem,
            smem,
            wide,
            pl.BlockSpec((1, local), lambda s: (0, 0)),
            one,
            pl.BlockSpec((1, pairs, 2, length, length), lambda s: (s, 0, 0, 0, 0)),
            one,
        ],
        out_specs=[
            wide,
            pl.BlockSpec((2 * pairs, 16, QUERY_TAPS * TILE), lambda s: (0, 0, 0)),
            pl.BlockSpec((1, TILE), lambda s: (0, 0)),
            pl.BlockSpec((1, local), lambda s: (0, 0)),
        ],
        out_shape=[
            jax.ShapeDtypeStruct(qkv.shape, bf16),
            jax.ShapeDtypeStruct((2 * pairs, 16, QUERY_TAPS * TILE), f32),
            jax.ShapeDtypeStruct((1, TILE), f32),
            jax.ShapeDtypeStruct((1, local), f32),
        ],
        scratch_shapes=[
            pltpu.VMEM((2, length + 2 * PAD, length), f32),
            pltpu.VMEM((2, length + 2 * PAD, length), bf16),
            pltpu.VMEM((2, length, length), bf16),
            pltpu.VMEM((length + TILE, length), bf16),
            pltpu.VMEM((2 * TILE, QUERY_TAPS * TILE), bf16),
            pltpu.VMEM((length, local), bf16),
            pltpu.VMEM((length, width), f32),
            pltpu.VMEM((2 * pairs, 2 * TILE, QUERY_TAPS * TILE), f32),
            pltpu.VMEM((length + TILE, span_pair), bf16),
            pltpu.VMEM((length + TILE, span_pair), f32),
        ],
        name="attend_bwd",
    )(kern, mix, qkv, gain, heads, probs, outer)


def xor_perm(count, bit):
    return [(index, index ^ bit) for index in range(count)]


def swap(value, axis, bit):
    return lax.ppermute(value, axis, xor_perm(lax.axis_size(axis), bit))


def batch_gather(value):
    return lax.all_gather(value, "batch", axis=0, tiled=True)


def batch_scatter(value):
    return lax.psum_scatter(value, "batch", scatter_dimension=0, tiled=True)


def ring_perms():
    count = lax.axis_size("seq")
    ahead = []
    for pair in range(lax.axis_size("batch") // 2):
        line = [2 * pair * count + index for index in range(count)]
        ring = line + [index + count for index in reversed(line)]
        ahead += [(here, ring[(step + 1) % len(ring)]) for step, here in enumerate(ring)]
    return ahead, [(there, here) for here, there in ahead]


def ring_side():
    return 1 - 2 * (lax.axis_index("batch") % 2)


def seq_gather(value, hops=None):
    count = lax.axis_size("seq")
    here = lax.axis_index("seq")
    side = ring_side()
    ahead, back = ring_perms()
    rows = value.shape[0]
    first, second = [value], [value]
    for _ in range(count - 1):
        first.append(lax.ppermute(first[-1], ("batch", "seq"), ahead))
        second.append(lax.ppermute(second[-1], ("batch", "seq"), back))
    if hops is not None:
        hops += [(one, two) for one, two in zip(first[1:], second[1:])]
    out = jnp.zeros((count * rows, value.shape[1]), value.dtype)
    out = lax.dynamic_update_slice(out, value, (here * rows, 0))
    for step in range(1, count):
        source = here - side * step
        near = jnp.logical_and(source >= 0, source < count)
        piece = jnp.where(near, first[step], second[count - step])
        out = lax.dynamic_update_slice(out, piece, ((source % count) * rows, 0))
    return out


def seq_scatter(value):
    count = lax.axis_size("seq")
    here = lax.axis_index("seq")
    side = ring_side()
    ahead, back = ring_perms()
    rows = value.shape[0] // count
    low, high = here == 0, here == count - 1
    skip_first = jnp.where(side > 0, low, high)
    skip_second = jnp.where(side > 0, high, low)

    def block(index):
        return lax.dynamic_slice_in_dim(value, jnp.clip(index, 0, count - 1) * rows, rows, 0)

    def came(piece, skip):
        return jnp.where(skip, 0.0, piece.astype(f32))

    first = second = None
    for step in range(1, count):
        far = side * (count - step)
        one, two = block(here + far), block(here - far)
        if first is not None:
            one = (one.astype(f32) + came(first, skip_first)).astype(bf16)
            two = (two.astype(f32) + came(second, skip_second)).astype(bf16)
        first = lax.ppermute(one, ("batch", "seq"), ahead)
        second = lax.ppermute(two, ("batch", "seq"), back)
    return block(here).astype(f32) + came(first, skip_first) + came(second, skip_second)


def seq_swap(blocks):
    count = lax.axis_size("seq")
    here = lax.axis_index("seq")
    out = jnp.zeros_like(blocks)
    own = lax.dynamic_index_in_dim(blocks, here, 0, True)
    out = lax.dynamic_update_slice_in_dim(out, own, here, 0)
    for step in range(1, count):
        piece = lax.dynamic_index_in_dim(blocks, (here + step) % count, 0, True)
        perm = [(index, (index + step) % count) for index in range(count)]
        piece = lax.ppermute(piece, "seq", perm)
        out = lax.dynamic_update_slice_in_dim(out, piece, (here - step) % count, 0)
    return out


def after(value, *others):
    return lax.optimization_barrier((value, *others))[0]


def all_sum(value, axes=("batch", "seq")):
    for axis in axes:
        bit = 1
        while bit < lax.axis_size(axis):
            value = value + swap(value, axis, bit)
            bit *= 2
    return value


def inverse_rms(values):
    return lax.rsqrt(jnp.mean(values * values, axis=-1, keepdims=True) + 1e-06)


def rms_back(values, inverse, inner):
    along = jnp.mean(values * inner, axis=-1, keepdims=True)
    return inverse * (inner - values * (inverse * inverse) * along)


def per_device(
    inputs,
    output_grad,
    source_tags,
    source_counts,
    gain_in,
    w_query,
    w_key,
    w_value,
    kernel,
    mixing,
    gain_head,
    w_out,
    gain_mid,
    w_gate,
    w_up,
    w_down,
):
    seqs, seg, width = inputs.shape
    parts = lax.axis_size("seq")
    lanes = lax.axis_size("batch")
    place_seq = lax.axis_index("seq")
    place_batch = lax.axis_index("batch")
    length = seg * parts
    groups = H // (2 * parts)
    local = groups * 2 * DH
    own = w_query.shape[0]
    blocks = parts * lanes

    gains = jnp.stack([gain_in, gain_head, gain_mid]).astype(f32)
    gains = lax.dynamic_update_slice_in_dim(
        jnp.zeros((3, width), f32), gains, (place_batch * parts + place_seq) * own, 1
    )
    gains = all_sum(gains.reshape(-1, 128), ("seq",))
    joint = jnp.stack([w_query, w_key, w_value], axis=1).reshape(own, 3, parts, local)
    joint = joint.transpose(2, 0, 1, 3).reshape(parts, own, 3 * local)
    joint = seq_swap(joint).reshape(parts * own, 3 * local)
    all_gains = all_sum(gains, ("batch",))
    hops = []
    x_all = [seq_gather(inputs[0], hops)]
    for index in range(1, seqs):
        x_all.append(seq_gather(after(inputs[index], hops[-2])))
    joint = after(joint, all_gains, hops[0])
    w_joint = batch_gather(joint)
    all_gains = all_gains.reshape(3, 1, width)
    gain_in32, gain_head32, gain_mid32 = all_gains[0], all_gains[1], all_gains[2]
    gain_own = lax.dynamic_slice_in_dim(gain_head32, place_seq * local, local, 1)
    kern_own = lax.dynamic_slice_in_dim(
        kernel.reshape(-1), place_seq * (2 * groups * QUERY_TAPS * KEY_TAPS), 2 * groups * QUERY_TAPS * KEY_TAPS, 0
    )
    mix_own = lax.dynamic_slice_in_dim(mixing.reshape(-1), place_seq * 4 * groups, 4 * groups, 0)

    order = [
        (index, (index % lanes) * parts + index // lanes) for index in range(blocks)
    ]
    w_join = batch_gather(lax.ppermute(after(w_out, x_all[0]), ("batch", "seq"), order))
    w_gate_up = batch_gather(jnp.concatenate([w_gate, w_up], axis=1))
    w_down_t = batch_gather(w_down.T)
    hidden_width = w_gate.shape[1]
    o_all = [lax.all_gather(output_grad[index], "seq", axis=0, tiled=True) for index in range(seqs)]

    source_ids = jnp.arange(source_counts.shape[0], dtype=jnp.int32)
    tag_count = jnp.sum(
        jnp.where(source_tags[:, None] == source_ids[None, :], source_counts[None, :], 0), axis=1
    )
    factor = length / tag_count.astype(f32)

    outputs, input_grads = [], []
    keep = []
    for index in range(seqs):
        x32 = x_all[index].astype(f32)
        x_inverse = inverse_rms(x32)
        normed = (x32 * x_inverse * gain_in32).astype(bf16)
        qkv = nn(normed, w_joint).astype(bf16)[None]
        joined, heads, probs = attend_fwd(kern_own, mix_own, qkv, gain_own)
        middle = inputs[index].astype(f32) + seq_scatter(nn(joined[0], w_join).astype(bf16))
        keep.append([x_inverse, normed, qkv, joined, heads, probs, middle])
    gain_mid_grad = jnp.zeros((1, width), f32)
    gain_in_grad = jnp.zeros((1, width), f32)
    ffn = []
    mid_parts = []
    results = []
    for index in range(seqs):
        middle = keep[index][-1]
        mid_inverse = inverse_rms(middle)
        n_all = seq_gather((middle * mid_inverse * gain_mid32).astype(bf16))
        both = nn(n_all, w_gate_up)
        gate, upward = both[:, :hidden_width], both[:, hidden_width:]
        sigma = 1.0 / (1.0 + jnp.exp(-gate))
        silu = gate * sigma
        hidden = (silu * upward).astype(bf16)
        down_in = (o_all[index].astype(f32) * factor[index]).astype(bf16)
        hidden_grad = nn(down_in, w_down_t)
        gate_grad = (hidden_grad * upward * (sigma * (1.0 + gate * (1.0 - sigma)))).astype(bf16)
        up_grad = (hidden_grad * silu).astype(bf16)
        grads = jnp.concatenate([gate_grad, up_grad], axis=1)
        mid_parts.append(seq_scatter(nt(grads, w_gate_up).astype(bf16)))
        ffn.append((n_all, hidden, down_in, grads))
    cat = lambda place: jnp.concatenate([item[place] for item in ffn], axis=0)
    all_n, all_hidden, all_down, all_grads = cat(0), cat(1), cat(2), cat(3)
    g_gate_up = tn(all_n, all_grads).astype(bf16)
    g_down_t = tn(all_down, all_hidden).astype(bf16)
    mid_parts = after(mid_parts, g_gate_up, g_down_t)
    g_gate_up = batch_scatter(g_gate_up)
    g_down_t = batch_scatter(g_down_t)
    for index in range(seqs):
        middle = keep[index][-1]
        mid_inverse = inverse_rms(middle)
        mid_grad = mid_parts[index]
        unit = middle * mid_inverse
        gain_mid_grad = gain_mid_grad + jnp.sum(mid_grad * unit, axis=0, keepdims=True)
        cotangent = output_grad[index].astype(f32) * factor[index]
        middle_grad = cotangent + rms_back(middle, mid_inverse, mid_grad * gain_mid32)
        a_all = seq_gather(after(middle_grad.astype(bf16), g_gate_up))
        keep[index] += [middle_grad, a_all]
        part = after(nt(ffn[index][1], w_down_t).astype(bf16), a_all)
        results.append(lax.psum_scatter(part, "seq", scatter_dimension=0, tiled=True))
    back = []
    for index in range(seqs):
        x_inverse, normed, qkv, joined, heads, probs, middle, middle_grad, a_all = keep[index]
        outer = nt(a_all, w_join)[None]
        outer = after(outer, n_part, results[0]) if back else after(outer, g_down_t)
        dqkv, corr, mix_sum, head_sum = attend_bwd(
            kern_own, mix_own, qkv, gain_own, heads, probs, outer
        )
        n_part = nt(dqkv[0], w_joint)
        unit_all = x_all[index].astype(f32) * x_inverse
        gain_in_grad = gain_in_grad + jnp.sum(n_part * unit_all, axis=0, keepdims=True)
        n_grad = seq_scatter(n_part.astype(bf16))
        x32 = inputs[index].astype(f32)
        inner = rms_back(x32, inverse_rms(x32), n_grad * gain_in32)
        input_grads.append((middle_grad + inner).astype(bf16))
        back.append((normed, dqkv[0], joined[0], a_all, corr, mix_sum, head_sum))
    cat = lambda place: jnp.concatenate([item[place] for item in back], axis=0)
    all_normed, all_dqkv, all_joined, all_a = cat(0), cat(1), cat(2), cat(3)
    all_dqkv = after(all_dqkv, results[-1])
    all_a = after(all_a, all_dqkv)
    for index in range(seqs):
        middle = after(keep[index][6], back[-1][1])
        outputs.append((middle + results[index].astype(f32)).astype(bf16))
    g_out = batch_scatter(tn(all_joined, all_a).astype(bf16))
    g_out = lax.ppermute(g_out, ("batch", "seq"), [(there, here) for here, there in order])
    g_out = g_out.astype(f32)
    g_joint = batch_scatter(tn(all_normed, all_dqkv).astype(bf16))
    g_joint = seq_swap(g_joint.reshape(parts, own, 3 * local)).astype(f32)
    g_joint = g_joint.reshape(parts, own, 3, local).transpose(2, 1, 0, 3).reshape(3, own, width)

    corr = sum(item[4] for item in back)
    mix_sum = sum(item[5] for item in back)
    head_sum = sum(item[6] for item in back)
    taps = corr[:, :KEY_TAPS].reshape(2 * groups, KEY_TAPS, QUERY_TAPS, TILE)
    kern_grad = taps.sum(-1).transpose(0, 2, 1)
    mix_grad = mix_sum[0, : 4 * groups]
    head_grad = head_sum[0]

    def spread(value, total):
        return lax.dynamic_update_slice_in_dim(
            jnp.zeros((total,), f32), value.reshape(-1), place_seq * value.size, 0
        )

    small = jnp.concatenate(
        [
            gain_in_grad[0],
            gain_mid_grad[0],
            spread(head_grad, width),
            spread(kern_grad, H * QUERY_TAPS * KEY_TAPS),
            spread(mix_grad, H * 2),
        ]
    )
    size = small.size
    small = jnp.pad(small, (0, -size % 1024)).reshape(-1, 128)
    small = all_sum(small).reshape(-1)
    start = (place_batch * parts + place_seq) * own
    cuts = [lax.dynamic_slice_in_dim(small, start + step * width, own, 0) for step in range(3)]
    kernel_sum = small[3 * width : 3 * width + H * QUERY_TAPS * KEY_TAPS].reshape(kernel.shape)
    mixing_sum = small[3 * width + H * QUERY_TAPS * KEY_TAPS : size].reshape(mixing.shape)
    return (
        jnp.stack(outputs),
        jnp.stack(input_grads),
        cuts[0],
        g_joint[0],
        g_joint[1],
        g_joint[2],
        kernel_sum,
        mixing_sum,
        cuts[2],
        g_out,
        cuts[1],
        g_gate_up[:, :hidden_width].astype(f32),
        g_gate_up[:, hidden_width:].astype(f32),
        g_down_t.T.astype(f32),
    )


def solution(mesh):
    rows = P(("batch", "seq"))
    mats = P(("batch", "seq"), None)
    tokens = P("batch", "seq", None)
    in_specs = (
        tokens,
        tokens,
        P("batch"),
        P(),
        rows,
        mats,
        mats,
        mats,
        P(),
        P(),
        rows,
        mats,
        rows,
        P("batch", "seq"),
        P("batch", "seq"),
        P("seq", "batch"),
    )
    out_specs = (
        tokens,
        tokens,
        rows,
        mats,
        mats,
        mats,
        P(),
        P(),
        rows,
        mats,
        rows,
        P("batch", "seq"),
        P("batch", "seq"),
        P("seq", "batch"),
    )
    return jax.shard_map(
        per_device, mesh=mesh, in_specs=in_specs, out_specs=out_specs, check_vma=False
    )
```

```python
import math

import jax
import jax.numpy as jnp
from jax import lax
from jax.experimental import pallas as pl
from jax.experimental.pallas import tpu as pltpu
from jax.sharding import PartitionSpec as P

H = 16
DH = 96
QUERY_TAPS = 6
KEY_TAPS = 11
REACH = KEY_TAPS // 2
TILE = 128
PAD = 16
bf16 = jnp.bfloat16
f32 = jnp.float32


def nn(left, right):
    return lax.dot_general(left, right, (((1,), (0,)), ((), ())), preferred_element_type=f32)


def nt(left, right):
    return lax.dot_general(left, right, (((1,), (1,)), ((), ())), preferred_element_type=f32)


def tn(left, right):
    return lax.dot_general(left, right, (((0,), (0,)), ((), ())), preferred_element_type=f32)


def lanes_of(begin, width):
    lane = lax.broadcasted_iota(jnp.int32, (1, width), 1)
    return jnp.logical_and(lane >= begin, lane < begin + DH).astype(f32)


def split(value):
    high = value.astype(bf16)
    return high, (value - high.astype(f32)).astype(bf16)


def fill_bands(kern_ref, base, bands, low_bands, offset):
    row = lax.broadcasted_iota(jnp.int32, (2 * TILE, TILE), 0)
    col = lax.broadcasted_iota(jnp.int32, (2 * TILE, TILE), 1)
    tap = offset(row, col)
    for lag in range(QUERY_TAPS):
        band = jnp.zeros((2 * TILE, TILE), f32)
        for key_lag in range(KEY_TAPS):
            band = jnp.where(tap == key_lag, kern_ref[base + lag * KEY_TAPS + key_lag], band)
        high, low = split(band)
        bands[:, lag * TILE : (lag + 1) * TILE] = high
        if low_bands is not None:
            low_bands[:, lag * TILE : (lag + 1) * TILE] = low


def valid_keys(first_query, rows, first_key):
    query = lax.broadcasted_iota(jnp.int32, (rows, TILE), 0) + first_query
    key = lax.broadcasted_iota(jnp.int32, (rows, TILE), 1) + (first_key - REACH)
    return jnp.logical_and(key >= 0, key <= query)


def shift_keys(keys, kx_ref):
    tail = jnp.zeros((TILE, keys.shape[1]), f32)
    moved = jnp.concatenate([keys.astype(f32), tail], axis=0)
    kx_ref[...] = pltpu.roll(moved, REACH, 0).astype(bf16)


def norm_parts(heads):
    masks = [lanes_of(head * DH, heads.shape[1]) for head in range(heads.shape[1] // DH)]
    means = jnp.zeros_like(heads)
    for mask in masks:
        means = means + mask * (jnp.sum(heads * mask, axis=1, keepdims=True) / DH)
    centred = heads - means
    inverse = jnp.zeros_like(heads)
    for mask in masks:
        spread = jnp.sum(centred * centred * mask, axis=1, keepdims=True) / DH
        inverse = inverse + mask * lax.rsqrt(spread + 1e-05)
    return centred, inverse, masks


def pair_slice(pair, local, part):
    span = min(2 * TILE, local)
    start = (3 * pair) // 2 * TILE
    if not isinstance(pair, int):
        start = pl.multiple_of(start, TILE)
    return pl.ds(part * local + start, span), pair * 2 * DH - start


def attend_fwd_body(
    kern_ref, mix_ref, qkv_ref, gain_ref,
    joined_ref, heads_ref, p_ref,
    high_ref, low_ref, bands_ref, low_bands_ref, kx_ref,
):
    length = qkv_ref.shape[1]
    local = heads_ref.shape[2]
    span_pair = kx_ref.shape[1]
    tiles = length // TILE
    pairs = local // (2 * DH)
    scale = 1.0 / math.sqrt(DH)

    @pl.when(pl.program_id(0) == 0)
    def _():
        high_ref[...] = jnp.zeros_like(high_ref)
        low_ref[...] = jnp.zeros_like(low_ref)

    heads_ref[...] = jnp.zeros_like(heads_ref)

    def one_pair(pair, carry):
        q_at, offset = pair_slice(pair, local, 0)
        k_at, _ = pair_slice(pair, local, 1)
        v_at, _ = pair_slice(pair, local, 2)
        h_at, _ = pair_slice(pair, local, 0)
        shift_keys(qkv_ref[0, :, k_at], kx_ref)

        def one_head(head, inner):
            base = (pair * 2 + head) * (QUERY_TAPS * KEY_TAPS)
            fill_bands(
                kern_ref, base, bands_ref, low_bands_ref, lambda row, col: (KEY_TAPS - 1) - (row - col)
            )
            query = qkv_ref[0, :, q_at] * lanes_of(offset + head * DH, span_pair).astype(bf16)
            for tile in range(tiles + 1):
                at = slice(tile * TILE, (tile + 1) * TILE)
                first = max(0, tile * TILE - PAD)
                scores = nt(query[first:], kx_ref[at, :]) * scale
                masked = jnp.where(valid_keys(first, length - first, tile * TILE), scores, 0.0)
                high, low = split(masked)
                high_ref[first + PAD :, at] = high
                low_ref[first + PAD :, at] = low
            for tile in range(tiles):
                first = tile * TILE
                high = high_ref[first:, first : first + 2 * TILE]
                low = low_ref[first:, first : first + 2 * TILE]
                bands = bands_ref[...]
                wide = nn(high, bands) + nn(low, bands) + nn(high, low_bands_ref[...])
                total = wide[:, :TILE]
                for lag in range(1, QUERY_TAPS):
                    total = total + pltpu.roll(wide[:, lag * TILE : (lag + 1) * TILE], lag, 0)
                p_ref[0, pair, head, first:, first : first + TILE] = total[PAD:]
            return inner

        lax.fori_loop(0, 2, one_head, 0)
        for tile in range(tiles):
            first = tile * TILE
            span = first + TILE
            query = lax.broadcasted_iota(jnp.int32, (TILE, span), 0) + first
            key = lax.broadcasted_iota(jnp.int32, (TILE, span), 1)
            valid = key <= query
            probs = []
            for head in range(2):
                logits = jnp.where(valid, p_ref[0, pair, head, first:span, :span], -1e30)
                top = jnp.max(logits, axis=1, keepdims=True)
                expon = jnp.where(valid, jnp.exp(logits - top), 0.0)
                prob = expon / jnp.sum(expon, axis=1, keepdims=True)
                p_ref[0, pair, head, first:span, :span] = prob
                probs.append(prob)
            out = heads_ref[0, first:span, h_at]
            for head in range(2):
                spot = (pair * 2 + head) * 2
                mixed = (mix_ref[spot] * probs[0] + mix_ref[spot + 1] * probs[1]).astype(bf16)
                mask = lanes_of(offset + head * DH, span_pair).astype(bf16)
                out = out + nn(mixed, qkv_ref[0, :span, v_at] * mask)
            heads_ref[0, first:span, h_at] = out
        return carry

    if pairs == 1:
        one_pair(0, 0)
    else:
        lax.fori_loop(0, pairs, one_pair, 0)
    for tile in range(tiles):
        at = slice(tile * TILE, (tile + 1) * TILE)
        centred, inverse, _ = norm_parts(heads_ref[0, at, :])
        joined_ref[0, at, :] = (centred * inverse * gain_ref[...]).astype(bf16)


def attend_bwd_body(
    kern_ref, mix_ref, qkv_ref, gain_ref, heads_ref, p_ref, dj_ref,
    dqkv_ref, gk_ref, gmix_ref, ggain_ref,
    d_ref, dlow_ref, mixed_ref, mt_ref, bands_ref, do_ref, acc_ref, corr_ref, kx_ref, dka_ref,
):
    length = qkv_ref.shape[1]
    local = heads_ref.shape[2]
    span_pair = kx_ref.shape[1]
    tiles = length // TILE
    pairs = local // (2 * DH)
    scale = 1.0 / math.sqrt(DH)
    lane = lax.broadcasted_iota(jnp.int32, (1, TILE), 1)

    @pl.when(pl.program_id(0) == 0)
    def _():
        d_ref[...] = jnp.zeros_like(d_ref)
        dlow_ref[...] = jnp.zeros_like(dlow_ref)
        mt_ref[...] = jnp.zeros_like(mt_ref)
        corr_ref[...] = jnp.zeros_like(corr_ref)
        gmix_ref[...] = jnp.zeros_like(gmix_ref)
        ggain_ref[...] = jnp.zeros_like(ggain_ref)

    gain_total = jnp.zeros((1, local), f32)
    for tile in range(tiles):
        at = slice(tile * TILE, (tile + 1) * TILE)
        centred, inverse, masks = norm_parts(heads_ref[0, at, :])
        unit = centred * inverse
        outer = dj_ref[0, at, :].astype(f32)
        gain_total = gain_total + jnp.sum(outer * unit, axis=0, keepdims=True)
        inner = outer * gain_ref[...]
        result = inner
        for mask in masks:
            mean = jnp.sum(inner * mask, axis=1, keepdims=True) / DH
            along = jnp.sum(inner * unit * mask, axis=1, keepdims=True) / DH
            result = result - mask * (mean + unit * along)
        do_ref[at, :] = (result * inverse).astype(bf16)
    ggain_ref[...] = ggain_ref[...] + gain_total
    acc_ref[...] = jnp.zeros_like(acc_ref)

    def one_pair(pair, carry):
        q_at, offset = pair_slice(pair, local, 0)
        k_at, _ = pair_slice(pair, local, 1)
        v_at, _ = pair_slice(pair, local, 2)
        h_at, _ = pair_slice(pair, local, 0)
        shift_keys(qkv_ref[0, :, k_at], kx_ref)
        dka_ref[...] = jnp.zeros_like(dka_ref)
        sums = [[jnp.zeros((1, 1), f32) for _ in range(2)] for _ in range(2)]
        mix = [[mix_ref[(pair * 2 + head) * 2 + other] for other in range(2)] for head in range(2)]
        head_masks = [lanes_of(offset + head * DH, span_pair).astype(bf16) for head in range(2)]
        for tile in range(tiles):
            first = tile * TILE
            span = first + TILE
            query = lax.broadcasted_iota(jnp.int32, (TILE, span), 0) + first
            valid = lax.broadcasted_iota(jnp.int32, (TILE, span), 1) <= query
            probs = [
                jnp.where(valid, p_ref[0, pair, head, first:span, :span], 0.0) for head in range(2)
            ]
            grads = []
            for head in range(2):
                mixed = (mix[head][0] * probs[0] + mix[head][1] * probs[1]).astype(bf16)
                mixed_ref[head, first:span, :span] = mixed
                grads.append(nt(do_ref[first:span, h_at] * head_masks[head], qkv_ref[0, :span, v_at]))
            for other in range(2):
                row_sum = jnp.zeros((TILE, 1), f32)
                for head in range(2):
                    along = jnp.sum(grads[head] * probs[other], axis=1, keepdims=True)
                    sums[head][other] = sums[head][other] + jnp.sum(along, axis=0, keepdims=True)
                    row_sum = row_sum + mix[head][other] * along
                outer = mix[0][other] * grads[0] + mix[1][other] * grads[1]
                inner = probs[other] * (outer - row_sum)
                d_ref[other, first + PAD : span + PAD, :span] = inner
                dlow_ref[other, first + PAD : span + PAD, :span] = inner.astype(bf16)
        spread = jnp.zeros((1, TILE), f32)
        for head in range(2):
            for other in range(2):
                spread = spread + jnp.where(
                    lane == pair * 4 + head * 2 + other, sums[head][other], 0.0
                )
        gmix_ref[...] = gmix_ref[...] + spread

        for tile in range(tiles):
            first = tile * TILE
            at = slice(first, first + TILE)
            total = acc_ref[at, v_at]
            for head in range(2):
                total = total + tn(mixed_ref[head, first:, at], do_ref[first:, h_at] * head_masks[head])
            acc_ref[at, v_at] = total

        def one_head(head, inner):
            base = (pair * 2 + head) * (QUERY_TAPS * KEY_TAPS)
            fill_bands(
                kern_ref, base, bands_ref, None, lambda row, col: row - TILE - col + (KEY_TAPS - 1)
            )
            lanes = lanes_of(offset + head * DH, span_pair).astype(bf16)
            query = qkv_ref[0, :, q_at] * lanes
            for tile in range(tiles + 1):
                start = max(0, tile - 1) * TILE
                at = slice(tile * TILE, (tile + 1) * TILE)
                scores = nt(kx_ref[at, :], query[start:]) * scale
                key = lax.broadcasted_iota(jnp.int32, (TILE, length - start), 0) + (tile * TILE - REACH)
                pos = lax.broadcasted_iota(jnp.int32, (TILE, length - start), 1) + start
                valid = jnp.logical_and(key >= 0, key <= pos)
                mt_ref[at, start:] = jnp.where(valid, scores, 0.0).astype(bf16)
            total_corr = corr_ref[pair * 2 + head]
            for tile in range(tiles):
                start = max(0, tile - 1) * TILE
                count = length - start
                source = d_ref[head, start + PAD :, tile * TILE : (tile + 1) * TILE]
                moved = [source[:count].astype(bf16)]
                for lag in range(1, QUERY_TAPS):
                    moved.append(pltpu.roll(source, source.shape[0] - lag, 0)[:count].astype(bf16))
                stacked = jnp.concatenate(moved, axis=1)
                total_corr = total_corr + nn(mt_ref[tile * TILE : (tile + 2) * TILE, start:], stacked)
            corr_ref[pair * 2 + head] = total_corr
            for tile in range(tiles + 1):
                first = tile * TILE
                at = slice(first, first + TILE)
                if tile == 0:
                    wide = nn(dlow_ref[head, first:, :TILE], bands_ref[TILE:, :])
                elif tile == tiles:
                    wide = nn(dlow_ref[head, first:, first - TILE : first], bands_ref[:TILE, :])
                else:
                    wide = nn(dlow_ref[head, first:, first - TILE : first + TILE], bands_ref[...])
                total = wide[:, :TILE]
                rows = wide.shape[0]
                for lag in range(1, QUERY_TAPS):
                    total = total + pltpu.roll(wide[:, lag * TILE : (lag + 1) * TILE], rows - lag, 0)
                begin = max(0, first - PAD)
                total = total[begin - (first - PAD) : rows - PAD]
                grad = jnp.where(valid_keys(begin, length - begin, first), total, 0.0).astype(bf16)
                acc_ref[begin:, q_at] = acc_ref[begin:, q_at] + nn(grad, kx_ref[at, :] * lanes) * scale
                dka_ref[at, :] = dka_ref[at, :] + tn(grad, query[begin:])
            return inner

        lax.fori_loop(0, 2, one_head, 0)
        keys = dka_ref[...]
        back = pltpu.roll(keys, keys.shape[0] - REACH, 0)[:length] * scale
        acc_ref[:, k_at] = acc_ref[:, k_at] + back
        return carry

    if pairs == 1:
        one_pair(0, 0)
    else:
        lax.fori_loop(0, pairs, one_pair, 0)
    dqkv_ref[0] = acc_ref[...].astype(bf16)

    @pl.when(pl.program_id(0) == pl.num_programs(0) - 1)
    def _():
        row = lax.broadcasted_iota(jnp.int32, (2 * TILE, QUERY_TAPS * TILE), 0)
        col = lax.broadcasted_iota(jnp.int32, (2 * TILE, QUERY_TAPS * TILE), 1) % TILE

        def one_head(head, carry):
            corr = corr_ref[head]
            taps = [
                jnp.sum(jnp.where(row - col == (KEY_TAPS - 1) - key_lag, corr, 0.0), axis=0, keepdims=True)
                for key_lag in range(KEY_TAPS)
            ]
            taps.append(jnp.zeros((16 - KEY_TAPS, QUERY_TAPS * TILE), f32))
            gk_ref[head] = jnp.concatenate(taps, axis=0)
            return carry

        lax.fori_loop(0, 2 * pairs, one_head, 0)


def attend_fwd(kern, mix, qkv, gain):
    seqs, length, width = qkv.shape
    local = width // 3
    pairs = local // (2 * DH)
    smem = pl.BlockSpec(memory_space=pltpu.SMEM)
    one = pl.BlockSpec((1, length, local), lambda s: (s, 0, 0))
    return pl.pallas_call(
        attend_fwd_body,
        grid=(seqs,),
        in_specs=[
            smem,
            smem,
            pl.BlockSpec((1, length, width), lambda s: (s, 0, 0)),
            pl.BlockSpec((1, local), lambda s: (0, 0)),
        ],
        out_specs=[one, one, pl.BlockSpec((1, pairs, 2, length, length), lambda s: (s, 0, 0, 0, 0))],
        out_shape=[
            jax.ShapeDtypeStruct((seqs, length, local), bf16),
            jax.ShapeDtypeStruct((seqs, length, local), f32),
            jax.ShapeDtypeStruct((seqs, pairs, 2, length, length), f32),
        ],
        scratch_shapes=[
            pltpu.VMEM((length + PAD, length + TILE), bf16),
            pltpu.VMEM((length + PAD, length + TILE), bf16),
            pltpu.VMEM((2 * TILE, QUERY_TAPS * TILE), bf16),
            pltpu.VMEM((2 * TILE, QUERY_TAPS * TILE), bf16),
            pltpu.VMEM((length + TILE, min(2 * TILE, local)), bf16),
        ],
        name="attend_fwd",
    )(kern, mix, qkv, gain)


def attend_bwd(kern, mix, qkv, gain, heads, probs, outer):
    seqs, length, width = qkv.shape
    local = width // 3
    pairs = local // (2 * DH)
    span_pair = min(2 * TILE, local)
    smem = pl.BlockSpec(memory_space=pltpu.SMEM)
    one = pl.BlockSpec((1, length, local), lambda s: (s, 0, 0))
    wide = pl.BlockSpec((1, length, width), lambda s: (s, 0, 0))
    return pl.pallas_call(
        attend_bwd_body,
        grid=(seqs,),
        in_specs=[
            smem,
            smem,
            wide,
            pl.BlockSpec((1, local), lambda s: (0, 0)),
            one,
            pl.BlockSpec((1, pairs, 2, length, length), lambda s: (s, 0, 0, 0, 0)),
            one,
        ],
        out_specs=[
            wide,
            pl.BlockSpec((2 * pairs, 16, QUERY_TAPS * TILE), lambda s: (0, 0, 0)),
            pl.BlockSpec((1, TILE), lambda s: (0, 0)),
            pl.BlockSpec((1, local), lambda s: (0, 0)),
        ],
        out_shape=[
            jax.ShapeDtypeStruct(qkv.shape, bf16),
            jax.ShapeDtypeStruct((2 * pairs, 16, QUERY_TAPS * TILE), f32),
            jax.ShapeDtypeStruct((1, TILE), f32),
            jax.ShapeDtypeStruct((1, local), f32),
        ],
        scratch_shapes=[
            pltpu.VMEM((2, length + 2 * PAD, length), f32),
            pltpu.VMEM((2, length + 2 * PAD, length), bf16),
            pltpu.VMEM((2, length, length), bf16),
            pltpu.VMEM((length + TILE, length), bf16),
            pltpu.VMEM((2 * TILE, QUERY_TAPS * TILE), bf16),
            pltpu.VMEM((length, local), bf16),
            pltpu.VMEM((length, width), f32),
            pltpu.VMEM((2 * pairs, 2 * TILE, QUERY_TAPS * TILE), f32),
            pltpu.VMEM((length + TILE, span_pair), bf16),
            pltpu.VMEM((length + TILE, span_pair), f32),
        ],
        name="attend_bwd",
    )(kern, mix, qkv, gain, heads, probs, outer)


def xor_perm(count, bit):
    return [(index, index ^ bit) for index in range(count)]


def swap(value, axis, bit):
    return lax.ppermute(value, axis, xor_perm(lax.axis_size(axis), bit))


def batch_gather(value):
    return lax.all_gather(value, "batch", axis=0, tiled=True)


def batch_scatter(value):
    return lax.psum_scatter(value, "batch", scatter_dimension=0, tiled=True)


def ring_perms():
    count = lax.axis_size("seq")
    ahead = []
    for pair in range(lax.axis_size("batch") // 2):
        line = [2 * pair * count + index for index in range(count)]
        ring = line + [index + count for index in reversed(line)]
        ahead += [(here, ring[(step + 1) % len(ring)]) for step, here in enumerate(ring)]
    return ahead, [(there, here) for here, there in ahead]


def ring_side():
    return 1 - 2 * (lax.axis_index("batch") % 2)


def seq_gather(value, hops=None, gates=None):
    count = lax.axis_size("seq")
    here = lax.axis_index("seq")
    side = ring_side()
    ahead, back = ring_perms()
    rows = value.shape[0]
    first, second = [value], [value]
    for step in range(count - 1):
        one, two = first[-1], second[-1]
        if gates is not None and step == count - 2:
            one, two = after((one, two), gates)
        first.append(lax.ppermute(one, ("batch", "seq"), ahead))
        second.append(lax.ppermute(two, ("batch", "seq"), back))
    if hops is not None:
        hops += [(one, two) for one, two in zip(first[1:], second[1:])]
    out = jnp.zeros((count * rows, value.shape[1]), value.dtype)
    out = lax.dynamic_update_slice(out, value, (here * rows, 0))
    for step in range(1, count):
        source = here - side * step
        near = jnp.logical_and(source >= 0, source < count)
        piece = jnp.where(near, first[step], second[count - step])
        out = lax.dynamic_update_slice(out, piece, ((source % count) * rows, 0))
    return out


def seq_scatter(value, hops=None):
    count = lax.axis_size("seq")
    here = lax.axis_index("seq")
    side = ring_side()
    ahead, back = ring_perms()
    rows = value.shape[0] // count
    low, high = here == 0, here == count - 1
    skip_first = jnp.where(side > 0, low, high)
    skip_second = jnp.where(side > 0, high, low)

    def block(index):
        return lax.dynamic_slice_in_dim(value, jnp.clip(index, 0, count - 1) * rows, rows, 0)

    def came(piece, skip):
        return jnp.where(skip, 0.0, piece.astype(f32))

    first = second = None
    for step in range(1, count):
        far = side * (count - step)
        one, two = block(here + far), block(here - far)
        if first is not None:
            one = (one.astype(f32) + came(first, skip_first)).astype(bf16)
            two = (two.astype(f32) + came(second, skip_second)).astype(bf16)
        first = lax.ppermute(one, ("batch", "seq"), ahead)
        second = lax.ppermute(two, ("batch", "seq"), back)
        if hops is not None:
            hops.append((first, second))
    return block(here).astype(f32) + came(first, skip_first) + came(second, skip_second)


def seq_swap(blocks):
    count = lax.axis_size("seq")
    here = lax.axis_index("seq")
    out = jnp.zeros_like(blocks)
    own = lax.dynamic_index_in_dim(blocks, here, 0, True)
    out = lax.dynamic_update_slice_in_dim(out, own, here, 0)
    for step in range(1, count):
        piece = lax.dynamic_index_in_dim(blocks, (here + step) % count, 0, True)
        perm = [(index, (index + step) % count) for index in range(count)]
        piece = lax.ppermute(piece, "seq", perm)
        out = lax.dynamic_update_slice_in_dim(out, piece, (here - step) % count, 0)
    return out


def after(value, *others):
    return lax.optimization_barrier((value, *others))[0]


def all_sum(value, axes=("batch", "seq")):
    for axis in axes:
        bit = 1
        while bit < lax.axis_size(axis):
            value = value + swap(value, axis, bit)
            bit *= 2
    return value


def inverse_rms(values):
    return lax.rsqrt(jnp.mean(values * values, axis=-1, keepdims=True) + 1e-06)


def rms_back(values, inverse, inner):
    along = jnp.mean(values * inner, axis=-1, keepdims=True)
    return inverse * (inner - values * (inverse * inverse) * along)


def per_device(
    inputs,
    output_grad,
    source_tags,
    source_counts,
    gain_in,
    w_query,
    w_key,
    w_value,
    kernel,
    mixing,
    gain_head,
    w_out,
    gain_mid,
    w_gate,
    w_up,
    w_down,
):
    seqs, seg, width = inputs.shape
    parts = lax.axis_size("seq")
    lanes = lax.axis_size("batch")
    place_seq = lax.axis_index("seq")
    place_batch = lax.axis_index("batch")
    length = seg * parts
    groups = H // (2 * parts)
    local = groups * 2 * DH
    own = w_query.shape[0]
    blocks = parts * lanes

    gains = jnp.stack([gain_in, gain_head, gain_mid]).astype(f32)
    gains = lax.dynamic_update_slice_in_dim(
        jnp.zeros((3, width), f32), gains, (place_batch * parts + place_seq) * own, 1
    )
    gains = all_sum(gains.reshape(-1, 128), ("seq",))
    joint = jnp.stack([w_query, w_key, w_value], axis=1).reshape(own, 3, parts, local)
    joint = joint.transpose(2, 0, 1, 3).reshape(parts, own, 3 * local)
    joint = seq_swap(joint).reshape(parts * own, 3 * local)
    all_gains = all_sum(gains, ("batch",))
    hops = []
    x_all = [seq_gather(inputs[0], hops)]
    order = [
        (index, (index % lanes) * parts + index // lanes) for index in range(blocks)
    ]
    out_rows = lax.ppermute(w_out, ("batch", "seq"), order)
    joint = after(joint, all_gains, hops[0], out_rows)
    w_joint = batch_gather(joint)
    all_gains = all_gains.reshape(3, 1, width)
    gain_in32, gain_head32, gain_mid32 = all_gains[0], all_gains[1], all_gains[2]
    gain_own = lax.dynamic_slice_in_dim(gain_head32, place_seq * local, local, 1)
    kern_own = lax.dynamic_slice_in_dim(
        kernel.reshape(-1), place_seq * (2 * groups * QUERY_TAPS * KEY_TAPS), 2 * groups * QUERY_TAPS * KEY_TAPS, 0
    )
    mix_own = lax.dynamic_slice_in_dim(mixing.reshape(-1), place_seq * 4 * groups, 4 * groups, 0)

    w_join = batch_gather(out_rows)
    w_gate_up = batch_gather(jnp.concatenate([w_gate, w_up], axis=1))
    w_down_t = batch_gather(w_down.T)
    hidden_width = w_gate.shape[1]
    o_all = [lax.all_gather(output_grad[index], "seq", axis=0, tiled=True) for index in range(seqs)]

    source_ids = jnp.arange(source_counts.shape[0], dtype=jnp.int32)
    tag_count = jnp.sum(
        jnp.where(source_tags[:, None] == source_ids[None, :], source_counts[None, :], 0), axis=1
    )
    factor = length / tag_count.astype(f32)

    outputs, input_grads = [], []
    keep = []
    for index in range(seqs):
        if index:
            x_all.append(seq_gather(after(inputs[index], hops[-2]), gates=qkv))
        x32 = x_all[index].astype(f32)
        x_inverse = inverse_rms(x32)
        normed = (x32 * x_inverse * gain_in32).astype(bf16)
        qkv = nn(normed, w_joint).astype(bf16)[None]
        joined, heads, probs = attend_fwd(kern_own, mix_own, qkv, gain_own)
        middle = inputs[index].astype(f32) + seq_scatter(nn(joined[0], w_join).astype(bf16))
        keep.append([x_inverse, normed, qkv, joined, heads, probs, middle])
    gain_mid_grad = jnp.zeros((1, width), f32)
    gain_in_grad = jnp.zeros((1, width), f32)
    ffn = []
    results = []
    n_all = []
    scattered = []
    gate_by = []
    mid_inverses = []
    for index in range(seqs):
        middle = keep[index][-1]
        mid_inverses.append(inverse_rms(middle))
        n_own = (middle * mid_inverses[-1] * gain_mid32).astype(bf16)
        n_all.append(seq_gather(n_own, gates=gate_by[-1] if gate_by else None))
        whole = after(n_all[index], ffn[-1][4]) if ffn else n_all[index]
        both = nn(whole, w_gate_up)
        gate_by.append(both)
        gate, upward = both[:, :hidden_width], both[:, hidden_width:]
        sigma = 1.0 / (1.0 + jnp.exp(-gate))
        silu = gate * sigma
        hidden = (silu * upward).astype(bf16)
        o_here = after(o_all[index], scattered[-1][0]) if scattered else o_all[index]
        down_in = (o_here.astype(f32) * factor[index]).astype(bf16)
        hidden_grad = nn(down_in, w_down_t)
        gate_grad = (hidden_grad * upward * (sigma * (1.0 + gate * (1.0 - sigma)))).astype(bf16)
        up_grad = (hidden_grad * silu).astype(bf16)
        grads = lax.optimization_barrier(jnp.concatenate([gate_grad, up_grad], axis=1))
        mid_part = nt(after(grads, scattered[-1][1]) if scattered else grads, w_gate_up)
        mid_part = mid_part.astype(bf16)
        ffn.append((n_all[index], hidden, down_in, grads, mid_part))
        scattered.append([])
        scattered[-1].append(seq_scatter(mid_part, scattered[-1]))
    cat = lambda place: jnp.concatenate([item[place] for item in ffn], axis=0)
    all_hidden, all_down = cat(1), cat(2)
    g_gate_up = sum(tn(item[0], item[3]) for item in ffn).astype(bf16)
    g_down_t = tn(after(all_down, g_gate_up, scattered[-1][0]), all_hidden).astype(bf16)
    outers = []
    for index in range(seqs):
        middle, mid_inverse = keep[index][-1], mid_inverses[index]
        mid_grad = after(scattered[index][-1], g_down_t if index else g_gate_up)
        unit = middle * mid_inverse
        gain_mid_grad = gain_mid_grad + jnp.sum(mid_grad * unit, axis=0, keepdims=True)
        cotangent = output_grad[index].astype(f32) * factor[index]
        middle_grad = cotangent + rms_back(middle, mid_inverse, mid_grad * gain_mid32)
        a_all = seq_gather(middle_grad.astype(bf16), gates=outers[-1] if outers else None)
        outers.append(nt(a_all, w_join))
        keep[index] += [middle_grad, a_all]
    g_gate_up = batch_scatter(g_gate_up)
    g_down_t = batch_scatter(g_down_t)
    parts_out = [nt(item[1], w_down_t).astype(bf16).reshape(parts, seg, width) for item in ffn]
    parts_out = jnp.concatenate(parts_out, axis=1).reshape(parts * seqs * seg, width)
    parts_out = after(parts_out, outers[0])
    results = lax.psum_scatter(parts_out, "seq", scatter_dimension=0, tiled=True)
    results = results.reshape(seqs, seg, width)
    back = []
    for index in range(seqs):
        x_inverse, normed, qkv, joined, heads, probs, middle, middle_grad, a_all = keep[index]
        outer = outers[index][None]
        outer = after(outer, n_part, g_gate_up) if back else outer
        dqkv, corr, mix_sum, head_sum = attend_bwd(
            kern_own, mix_own, qkv, gain_own, heads, probs, outer
        )
        n_part = nt(after(dqkv, g_down_t)[0] if back else dqkv[0], w_joint)
        unit_all = x_all[index].astype(f32) * x_inverse
        gain_in_grad = gain_in_grad + jnp.sum(n_part * unit_all, axis=0, keepdims=True)
        n_grad = seq_scatter(n_part.astype(bf16))
        x32 = inputs[index].astype(f32)
        inner = rms_back(x32, inverse_rms(x32), n_grad * gain_in32)
        input_grads.append((middle_grad + inner).astype(bf16))
        back.append((normed, dqkv[0], joined[0], a_all, corr, mix_sum, head_sum))
    cat = lambda place: jnp.concatenate([item[place] for item in back], axis=0)
    all_normed, all_dqkv, all_joined, all_a = cat(0), cat(1), cat(2), cat(3)
    g_joint = tn(all_normed, all_dqkv).astype(bf16)
    for index in range(seqs):
        middle = after(keep[index][6], back[-1][1])
        outputs.append((middle + results[index].astype(f32)).astype(bf16))
    g_out = tn(all_joined, all_a).astype(bf16)
    span = parts * own
    packed = [g_joint.reshape(lanes, span, 3 * local), g_out.reshape(lanes, -1, 3 * local)]
    packed = batch_scatter(jnp.concatenate(packed, axis=1).reshape(-1, 3 * local))
    g_out = packed[span:].reshape(own, width)
    g_out = lax.ppermute(g_out, ("batch", "seq"), [(there, here) for here, there in order])
    g_out = g_out.astype(f32)
    g_joint = seq_swap(packed[:span].reshape(parts, own, 3 * local)).astype(f32)
    g_joint = g_joint.reshape(parts, own, 3, local).transpose(2, 1, 0, 3).reshape(3, own, width)

    corr = sum(item[4] for item in back)
    mix_sum = sum(item[5] for item in back)
    head_sum = sum(item[6] for item in back)
    taps = corr[:, :KEY_TAPS].reshape(2 * groups, KEY_TAPS, QUERY_TAPS, TILE)
    kern_grad = taps.sum(-1).transpose(0, 2, 1)
    mix_grad = mix_sum[0, : 4 * groups]
    head_grad = head_sum[0]

    def spread(value, total):
        return lax.dynamic_update_slice_in_dim(
            jnp.zeros((total,), f32), value.reshape(-1), place_seq * value.size, 0
        )

    small = jnp.concatenate(
        [
            gain_in_grad[0],
            gain_mid_grad[0],
            spread(head_grad, width),
            spread(kern_grad, H * QUERY_TAPS * KEY_TAPS),
            spread(mix_grad, H * 2),
        ]
    )
    size = small.size
    small = jnp.pad(small, (0, -size % 1024)).reshape(-1, 128)
    small = all_sum(small).reshape(-1)
    start = (place_batch * parts + place_seq) * own
    cuts = [lax.dynamic_slice_in_dim(small, start + step * width, own, 0) for step in range(3)]
    kernel_sum = small[3 * width : 3 * width + H * QUERY_TAPS * KEY_TAPS].reshape(kernel.shape)
    mixing_sum = small[3 * width + H * QUERY_TAPS * KEY_TAPS : size].reshape(mixing.shape)
    return (
        jnp.stack(outputs),
        jnp.stack(input_grads),
        cuts[0],
        g_joint[0],
        g_joint[1],
        g_joint[2],
        kernel_sum,
        mixing_sum,
        cuts[2],
        g_out,
        cuts[1],
        g_gate_up[:, :hidden_width].astype(f32),
        g_gate_up[:, hidden_width:].astype(f32),
        g_down_t.T.astype(f32),
    )


def solution(mesh):
    rows = P(("batch", "seq"))
    mats = P(("batch", "seq"), None)
    tokens = P("batch", "seq", None)
    in_specs = (
        tokens,
        tokens,
        P("batch"),
        P(),
        rows,
        mats,
        mats,
        mats,
        P(),
        P(),
        rows,
        mats,
        rows,
        P("batch", "seq"),
        P("batch", "seq"),
        P("seq", "batch"),
    )
    out_specs = (
        tokens,
        tokens,
        rows,
        mats,
        mats,
        mats,
        P(),
        P(),
        rows,
        mats,
        rows,
        P("batch", "seq"),
        P("batch", "seq"),
        P("seq", "batch"),
    )
    return jax.shard_map(
        per_device, mesh=mesh, in_specs=in_specs, out_specs=out_specs, check_vma=False
    )
```

```python
import math

import jax
import jax.numpy as jnp
from jax import lax
from jax.experimental import pallas as pl
from jax.experimental.pallas import tpu as pltpu
from jax.sharding import PartitionSpec as P

H = 16
DH = 96
QUERY_TAPS = 6
KEY_TAPS = 11
REACH = KEY_TAPS // 2
TILE = 128
PAD = 16
bf16 = jnp.bfloat16
f32 = jnp.float32


def nn(left, right):
    return lax.dot_general(left, right, (((1,), (0,)), ((), ())), preferred_element_type=f32)


def nt(left, right):
    return lax.dot_general(left, right, (((1,), (1,)), ((), ())), preferred_element_type=f32)


def tn(left, right):
    return lax.dot_general(left, right, (((0,), (0,)), ((), ())), preferred_element_type=f32)


def lanes_of(begin, width):
    lane = lax.broadcasted_iota(jnp.int32, (1, width), 1)
    return jnp.logical_and(lane >= begin, lane < begin + DH).astype(f32)


def split(value):
    high = value.astype(bf16)
    return high, (value - high.astype(f32)).astype(bf16)


def fill_bands(kern_ref, base, bands, low_bands, offset):
    row = lax.broadcasted_iota(jnp.int32, (2 * TILE, TILE), 0)
    col = lax.broadcasted_iota(jnp.int32, (2 * TILE, TILE), 1)
    tap = offset(row, col)
    for lag in range(QUERY_TAPS):
        band = jnp.zeros((2 * TILE, TILE), f32)
        for key_lag in range(KEY_TAPS):
            band = jnp.where(tap == key_lag, kern_ref[base + lag * KEY_TAPS + key_lag], band)
        high, low = split(band)
        bands[:, lag * TILE : (lag + 1) * TILE] = high
        if low_bands is not None:
            low_bands[:, lag * TILE : (lag + 1) * TILE] = low


def valid_keys(first_query, rows, first_key):
    query = lax.broadcasted_iota(jnp.int32, (rows, TILE), 0) + first_query
    key = lax.broadcasted_iota(jnp.int32, (rows, TILE), 1) + (first_key - REACH)
    return jnp.logical_and(key >= 0, key <= query)


def shift_keys(keys, kx_ref):
    tail = jnp.zeros((TILE, keys.shape[1]), f32)
    moved = jnp.concatenate([keys.astype(f32), tail], axis=0)
    kx_ref[...] = pltpu.roll(moved, REACH, 0).astype(bf16)


def norm_parts(heads):
    masks = [lanes_of(head * DH, heads.shape[1]) for head in range(heads.shape[1] // DH)]
    means = jnp.zeros_like(heads)
    for mask in masks:
        means = means + mask * (jnp.sum(heads * mask, axis=1, keepdims=True) / DH)
    centred = heads - means
    inverse = jnp.zeros_like(heads)
    for mask in masks:
        spread = jnp.sum(centred * centred * mask, axis=1, keepdims=True) / DH
        inverse = inverse + mask * lax.rsqrt(spread + 1e-05)
    return centred, inverse, masks


def pair_slice(pair, local, part):
    span = min(2 * TILE, local)
    start = (3 * pair) // 2 * TILE
    if not isinstance(pair, int):
        start = pl.multiple_of(start, TILE)
    return pl.ds(part * local + start, span), pair * 2 * DH - start


def attend_fwd_body(
    kern_ref, mix_ref, qkv_ref, gain_ref,
    joined_ref, heads_ref, p_ref,
    high_ref, low_ref, bands_ref, low_bands_ref, kx_ref,
):
    length = qkv_ref.shape[1]
    local = heads_ref.shape[2]
    span_pair = kx_ref.shape[1]
    tiles = length // TILE
    pairs = local // (2 * DH)
    scale = 1.0 / math.sqrt(DH)

    @pl.when(pl.program_id(0) == 0)
    def _():
        high_ref[...] = jnp.zeros_like(high_ref)
        low_ref[...] = jnp.zeros_like(low_ref)

    heads_ref[...] = jnp.zeros_like(heads_ref)

    def one_pair(pair, carry):
        q_at, offset = pair_slice(pair, local, 0)
        k_at, _ = pair_slice(pair, local, 1)
        v_at, _ = pair_slice(pair, local, 2)
        h_at, _ = pair_slice(pair, local, 0)
        shift_keys(qkv_ref[0, :, k_at], kx_ref)

        def one_head(head, inner):
            base = (pair * 2 + head) * (QUERY_TAPS * KEY_TAPS)
            fill_bands(
                kern_ref, base, bands_ref, low_bands_ref, lambda row, col: (KEY_TAPS - 1) - (row - col)
            )
            query = qkv_ref[0, :, q_at] * lanes_of(offset + head * DH, span_pair).astype(bf16)
            for tile in range(tiles + 1):
                at = slice(tile * TILE, (tile + 1) * TILE)
                first = max(0, tile * TILE - PAD)
                scores = nt(query[first:], kx_ref[at, :]) * scale
                masked = jnp.where(valid_keys(first, length - first, tile * TILE), scores, 0.0)
                high, low = split(masked)
                high_ref[first + PAD :, at] = high
                low_ref[first + PAD :, at] = low
            for tile in range(tiles):
                first = tile * TILE
                high = high_ref[first:, first : first + 2 * TILE]
                low = low_ref[first:, first : first + 2 * TILE]
                bands = bands_ref[...]
                wide = nn(high, bands) + nn(low, bands) + nn(high, low_bands_ref[...])
                total = wide[:, :TILE]
                for lag in range(1, QUERY_TAPS):
                    total = total + pltpu.roll(wide[:, lag * TILE : (lag + 1) * TILE], lag, 0)
                p_ref[0, pair, head, first:, first : first + TILE] = total[PAD:]
            return inner

        lax.fori_loop(0, 2, one_head, 0)
        for tile in range(tiles):
            first = tile * TILE
            span = first + TILE
            query = lax.broadcasted_iota(jnp.int32, (TILE, span), 0) + first
            key = lax.broadcasted_iota(jnp.int32, (TILE, span), 1)
            valid = key <= query
            probs = []
            for head in range(2):
                logits = jnp.where(valid, p_ref[0, pair, head, first:span, :span], -1e30)
                top = jnp.max(logits, axis=1, keepdims=True)
                expon = jnp.where(valid, jnp.exp(logits - top), 0.0)
                prob = expon / jnp.sum(expon, axis=1, keepdims=True)
                p_ref[0, pair, head, first:span, :span] = prob
                probs.append(prob)
            out = heads_ref[0, first:span, h_at]
            for head in range(2):
                spot = (pair * 2 + head) * 2
                mixed = (mix_ref[spot] * probs[0] + mix_ref[spot + 1] * probs[1]).astype(bf16)
                mask = lanes_of(offset + head * DH, span_pair).astype(bf16)
                out = out + nn(mixed, qkv_ref[0, :span, v_at] * mask)
            heads_ref[0, first:span, h_at] = out
        return carry

    if pairs == 1:
        one_pair(0, 0)
    else:
        lax.fori_loop(0, pairs, one_pair, 0)
    for tile in range(tiles):
        at = slice(tile * TILE, (tile + 1) * TILE)
        centred, inverse, _ = norm_parts(heads_ref[0, at, :])
        joined_ref[0, at, :] = (centred * inverse * gain_ref[...]).astype(bf16)


def attend_bwd_body(
    kern_ref, mix_ref, qkv_ref, gain_ref, heads_ref, p_ref, dj_ref,
    dqkv_ref, gk_ref, gmix_ref, ggain_ref,
    d_ref, dlow_ref, mixed_ref, mt_ref, bands_ref, do_ref, acc_ref, corr_ref, kx_ref, dka_ref,
):
    length = qkv_ref.shape[1]
    local = heads_ref.shape[2]
    span_pair = kx_ref.shape[1]
    tiles = length // TILE
    pairs = local // (2 * DH)
    scale = 1.0 / math.sqrt(DH)
    lane = lax.broadcasted_iota(jnp.int32, (1, TILE), 1)

    @pl.when(pl.program_id(0) == 0)
    def _():
        d_ref[...] = jnp.zeros_like(d_ref)
        dlow_ref[...] = jnp.zeros_like(dlow_ref)
        mt_ref[...] = jnp.zeros_like(mt_ref)
        corr_ref[...] = jnp.zeros_like(corr_ref)
        gmix_ref[...] = jnp.zeros_like(gmix_ref)
        ggain_ref[...] = jnp.zeros_like(ggain_ref)

    gain_total = jnp.zeros((1, local), f32)
    for tile in range(tiles):
        at = slice(tile * TILE, (tile + 1) * TILE)
        centred, inverse, masks = norm_parts(heads_ref[0, at, :])
        unit = centred * inverse
        outer = dj_ref[0, at, :].astype(f32)
        gain_total = gain_total + jnp.sum(outer * unit, axis=0, keepdims=True)
        inner = outer * gain_ref[...]
        result = inner
        for mask in masks:
            mean = jnp.sum(inner * mask, axis=1, keepdims=True) / DH
            along = jnp.sum(inner * unit * mask, axis=1, keepdims=True) / DH
            result = result - mask * (mean + unit * along)
        do_ref[at, :] = (result * inverse).astype(bf16)
    ggain_ref[...] = ggain_ref[...] + gain_total
    acc_ref[...] = jnp.zeros_like(acc_ref)

    def one_pair(pair, carry):
        q_at, offset = pair_slice(pair, local, 0)
        k_at, _ = pair_slice(pair, local, 1)
        v_at, _ = pair_slice(pair, local, 2)
        h_at, _ = pair_slice(pair, local, 0)
        shift_keys(qkv_ref[0, :, k_at], kx_ref)
        dka_ref[...] = jnp.zeros_like(dka_ref)
        sums = [[jnp.zeros((1, 1), f32) for _ in range(2)] for _ in range(2)]
        mix = [[mix_ref[(pair * 2 + head) * 2 + other] for other in range(2)] for head in range(2)]
        head_masks = [lanes_of(offset + head * DH, span_pair).astype(bf16) for head in range(2)]
        for tile in range(tiles):
            first = tile * TILE
            span = first + TILE
            query = lax.broadcasted_iota(jnp.int32, (TILE, span), 0) + first
            valid = lax.broadcasted_iota(jnp.int32, (TILE, span), 1) <= query
            probs = [
                jnp.where(valid, p_ref[0, pair, head, first:span, :span], 0.0) for head in range(2)
            ]
            grads = []
            for head in range(2):
                mixed = (mix[head][0] * probs[0] + mix[head][1] * probs[1]).astype(bf16)
                mixed_ref[head, first:span, :span] = mixed
                grads.append(nt(do_ref[first:span, h_at] * head_masks[head], qkv_ref[0, :span, v_at]))
            for other in range(2):
                row_sum = jnp.zeros((TILE, 1), f32)
                for head in range(2):
                    along = jnp.sum(grads[head] * probs[other], axis=1, keepdims=True)
                    sums[head][other] = sums[head][other] + jnp.sum(along, axis=0, keepdims=True)
                    row_sum = row_sum + mix[head][other] * along
                outer = mix[0][other] * grads[0] + mix[1][other] * grads[1]
                inner = probs[other] * (outer - row_sum)
                d_ref[other, first + PAD : span + PAD, :span] = inner
                dlow_ref[other, first + PAD : span + PAD, :span] = inner.astype(bf16)
        spread = jnp.zeros((1, TILE), f32)
        for head in range(2):
            for other in range(2):
                spread = spread + jnp.where(
                    lane == pair * 4 + head * 2 + other, sums[head][other], 0.0
                )
        gmix_ref[...] = gmix_ref[...] + spread

        for tile in range(tiles):
            first = tile * TILE
            at = slice(first, first + TILE)
            total = acc_ref[at, v_at]
            for head in range(2):
                total = total + tn(mixed_ref[head, first:, at], do_ref[first:, h_at] * head_masks[head])
            acc_ref[at, v_at] = total

        def one_head(head, inner):
            base = (pair * 2 + head) * (QUERY_TAPS * KEY_TAPS)
            fill_bands(
                kern_ref, base, bands_ref, None, lambda row, col: row - TILE - col + (KEY_TAPS - 1)
            )
            lanes = lanes_of(offset + head * DH, span_pair).astype(bf16)
            query = qkv_ref[0, :, q_at] * lanes
            for tile in range(tiles + 1):
                start = max(0, tile - 1) * TILE
                at = slice(tile * TILE, (tile + 1) * TILE)
                scores = nt(kx_ref[at, :], query[start:]) * scale
                key = lax.broadcasted_iota(jnp.int32, (TILE, length - start), 0) + (tile * TILE - REACH)
                pos = lax.broadcasted_iota(jnp.int32, (TILE, length - start), 1) + start
                valid = jnp.logical_and(key >= 0, key <= pos)
                mt_ref[at, start:] = jnp.where(valid, scores, 0.0).astype(bf16)
            total_corr = corr_ref[pair * 2 + head]
            for tile in range(tiles):
                start = max(0, tile - 1) * TILE
                count = length - start
                source = d_ref[head, start + PAD :, tile * TILE : (tile + 1) * TILE]
                moved = [source[:count].astype(bf16)]
                for lag in range(1, QUERY_TAPS):
                    moved.append(pltpu.roll(source, source.shape[0] - lag, 0)[:count].astype(bf16))
                stacked = jnp.concatenate(moved, axis=1)
                total_corr = total_corr + nn(mt_ref[tile * TILE : (tile + 2) * TILE, start:], stacked)
            corr_ref[pair * 2 + head] = total_corr
            for tile in range(tiles + 1):
                first = tile * TILE
                at = slice(first, first + TILE)
                if tile == 0:
                    wide = nn(dlow_ref[head, first:, :TILE], bands_ref[TILE:, :])
                elif tile == tiles:
                    wide = nn(dlow_ref[head, first:, first - TILE : first], bands_ref[:TILE, :])
                else:
                    wide = nn(dlow_ref[head, first:, first - TILE : first + TILE], bands_ref[...])
                total = wide[:, :TILE]
                rows = wide.shape[0]
                for lag in range(1, QUERY_TAPS):
                    total = total + pltpu.roll(wide[:, lag * TILE : (lag + 1) * TILE], rows - lag, 0)
                begin = max(0, first - PAD)
                total = total[begin - (first - PAD) : rows - PAD]
                grad = jnp.where(valid_keys(begin, length - begin, first), total, 0.0).astype(bf16)
                acc_ref[begin:, q_at] = acc_ref[begin:, q_at] + nn(grad, kx_ref[at, :] * lanes) * scale
                dka_ref[at, :] = dka_ref[at, :] + tn(grad, query[begin:])
            return inner

        lax.fori_loop(0, 2, one_head, 0)
        keys = dka_ref[...]
        back = pltpu.roll(keys, keys.shape[0] - REACH, 0)[:length] * scale
        acc_ref[:, k_at] = acc_ref[:, k_at] + back
        return carry

    if pairs == 1:
        one_pair(0, 0)
    else:
        lax.fori_loop(0, pairs, one_pair, 0)
    dqkv_ref[0] = acc_ref[...].astype(bf16)

    @pl.when(pl.program_id(0) == pl.num_programs(0) - 1)
    def _():
        row = lax.broadcasted_iota(jnp.int32, (2 * TILE, QUERY_TAPS * TILE), 0)
        col = lax.broadcasted_iota(jnp.int32, (2 * TILE, QUERY_TAPS * TILE), 1) % TILE

        def one_head(head, carry):
            corr = corr_ref[head]
            taps = [
                jnp.sum(jnp.where(row - col == (KEY_TAPS - 1) - key_lag, corr, 0.0), axis=0, keepdims=True)
                for key_lag in range(KEY_TAPS)
            ]
            taps.append(jnp.zeros((16 - KEY_TAPS, QUERY_TAPS * TILE), f32))
            gk_ref[head] = jnp.concatenate(taps, axis=0)
            return carry

        lax.fori_loop(0, 2 * pairs, one_head, 0)


def attend_fwd(kern, mix, qkv, gain):
    seqs, length, width = qkv.shape
    local = width // 3
    pairs = local // (2 * DH)
    smem = pl.BlockSpec(memory_space=pltpu.SMEM)
    one = pl.BlockSpec((1, length, local), lambda s: (s, 0, 0))
    return pl.pallas_call(
        attend_fwd_body,
        grid=(seqs,),
        in_specs=[
            smem,
            smem,
            pl.BlockSpec((1, length, width), lambda s: (s, 0, 0)),
            pl.BlockSpec((1, local), lambda s: (0, 0)),
        ],
        out_specs=[one, one, pl.BlockSpec((1, pairs, 2, length, length), lambda s: (s, 0, 0, 0, 0))],
        out_shape=[
            jax.ShapeDtypeStruct((seqs, length, local), bf16),
            jax.ShapeDtypeStruct((seqs, length, local), f32),
            jax.ShapeDtypeStruct((seqs, pairs, 2, length, length), f32),
        ],
        scratch_shapes=[
            pltpu.VMEM((length + PAD, length + TILE), bf16),
            pltpu.VMEM((length + PAD, length + TILE), bf16),
            pltpu.VMEM((2 * TILE, QUERY_TAPS * TILE), bf16),
            pltpu.VMEM((2 * TILE, QUERY_TAPS * TILE), bf16),
            pltpu.VMEM((length + TILE, min(2 * TILE, local)), bf16),
        ],
        name="attend_fwd",
    )(kern, mix, qkv, gain)


def attend_bwd(kern, mix, qkv, gain, heads, probs, outer):
    seqs, length, width = qkv.shape
    local = width // 3
    pairs = local // (2 * DH)
    span_pair = min(2 * TILE, local)
    smem = pl.BlockSpec(memory_space=pltpu.SMEM)
    one = pl.BlockSpec((1, length, local), lambda s: (s, 0, 0))
    wide = pl.BlockSpec((1, length, width), lambda s: (s, 0, 0))
    return pl.pallas_call(
        attend_bwd_body,
        grid=(seqs,),
        in_specs=[
            smem,
            smem,
            wide,
            pl.BlockSpec((1, local), lambda s: (0, 0)),
            one,
            pl.BlockSpec((1, pairs, 2, length, length), lambda s: (s, 0, 0, 0, 0)),
            one,
        ],
        out_specs=[
            wide,
            pl.BlockSpec((2 * pairs, 16, QUERY_TAPS * TILE), lambda s: (0, 0, 0)),
            pl.BlockSpec((1, TILE), lambda s: (0, 0)),
            pl.BlockSpec((1, local), lambda s: (0, 0)),
        ],
        out_shape=[
            jax.ShapeDtypeStruct(qkv.shape, bf16),
            jax.ShapeDtypeStruct((2 * pairs, 16, QUERY_TAPS * TILE), f32),
            jax.ShapeDtypeStruct((1, TILE), f32),
            jax.ShapeDtypeStruct((1, local), f32),
        ],
        scratch_shapes=[
            pltpu.VMEM((2, length + 2 * PAD, length), f32),
            pltpu.VMEM((2, length + 2 * PAD, length), bf16),
            pltpu.VMEM((2, length, length), bf16),
            pltpu.VMEM((length + TILE, length), bf16),
            pltpu.VMEM((2 * TILE, QUERY_TAPS * TILE), bf16),
            pltpu.VMEM((length, local), bf16),
            pltpu.VMEM((length, width), f32),
            pltpu.VMEM((2 * pairs, 2 * TILE, QUERY_TAPS * TILE), f32),
            pltpu.VMEM((length + TILE, span_pair), bf16),
            pltpu.VMEM((length + TILE, span_pair), f32),
        ],
        name="attend_bwd",
    )(kern, mix, qkv, gain, heads, probs, outer)


def xor_perm(count, bit):
    return [(index, index ^ bit) for index in range(count)]


def swap(value, axis, bit):
    return lax.ppermute(value, axis, xor_perm(lax.axis_size(axis), bit))


def batch_gather(value):
    return lax.all_gather(value, "batch", axis=0, tiled=True)


def batch_scatter(value):
    return lax.psum_scatter(value, "batch", scatter_dimension=0, tiled=True)


def ring_perms():
    count = lax.axis_size("seq")
    ahead = []
    for pair in range(lax.axis_size("batch") // 2):
        line = [2 * pair * count + index for index in range(count)]
        ring = line + [index + count for index in reversed(line)]
        ahead += [(here, ring[(step + 1) % len(ring)]) for step, here in enumerate(ring)]
    return ahead, [(there, here) for here, there in ahead]


def ring_side():
    return 1 - 2 * (lax.axis_index("batch") % 2)


def seq_gather(value, hops=None, gates=None):
    count = lax.axis_size("seq")
    here = lax.axis_index("seq")
    side = ring_side()
    ahead, back = ring_perms()
    rows = value.shape[0]
    first, second = [value], [value]
    for step in range(count - 1):
        one, two = first[-1], second[-1]
        if gates is not None and step == count - 2:
            one, two = after((one, two), gates)
        first.append(lax.ppermute(one, ("batch", "seq"), ahead))
        second.append(lax.ppermute(two, ("batch", "seq"), back))
    if hops is not None:
        hops += [(one, two) for one, two in zip(first[1:], second[1:])]
    out = jnp.broadcast_to(value[None], (count, *value.shape)).reshape(count * rows, -1)
    for step in range(1, count):
        source = here - side * step
        near = jnp.logical_and(source >= 0, source < count)
        piece = jnp.where(near, first[step], second[count - step])
        out = lax.dynamic_update_slice(out, piece, ((source % count) * rows, 0))
    return out


def seq_scatter(value, hops=None):
    count = lax.axis_size("seq")
    here = lax.axis_index("seq")
    side = ring_side()
    ahead, back = ring_perms()
    rows = value.shape[0] // count
    low, high = here == 0, here == count - 1
    skip_first = jnp.where(side > 0, low, high)
    skip_second = jnp.where(side > 0, high, low)

    def block(index):
        return lax.dynamic_slice_in_dim(value, jnp.clip(index, 0, count - 1) * rows, rows, 0)

    def came(piece, skip):
        return jnp.where(skip, 0.0, piece.astype(f32))

    first = second = None
    for step in range(1, count):
        far = side * (count - step)
        one, two = block(here + far), block(here - far)
        if first is not None:
            one = (one.astype(f32) + came(first, skip_first)).astype(bf16)
            two = (two.astype(f32) + came(second, skip_second)).astype(bf16)
        first = lax.ppermute(one, ("batch", "seq"), ahead)
        second = lax.ppermute(two, ("batch", "seq"), back)
        if hops is not None:
            hops.append((first, second))
    return block(here).astype(f32) + came(first, skip_first) + came(second, skip_second)


def seq_swap(blocks):
    count = lax.axis_size("seq")
    here = lax.axis_index("seq")
    out = jnp.zeros_like(blocks)
    own = lax.dynamic_index_in_dim(blocks, here, 0, True)
    out = lax.dynamic_update_slice_in_dim(out, own, here, 0)
    for step in range(1, count):
        piece = lax.dynamic_index_in_dim(blocks, (here + step) % count, 0, True)
        perm = [(index, (index + step) % count) for index in range(count)]
        piece = lax.ppermute(piece, "seq", perm)
        out = lax.dynamic_update_slice_in_dim(out, piece, (here - step) % count, 0)
    return out


def after(value, *others):
    return lax.optimization_barrier((value, *others))[0]


def all_sum(value, axes=("batch", "seq")):
    for axis in axes:
        bit = 1
        while bit < lax.axis_size(axis):
            value = value + swap(value, axis, bit)
            bit *= 2
    return value


def inverse_rms(values):
    return lax.rsqrt(jnp.mean(values * values, axis=-1, keepdims=True) + 1e-06)


def rms_back(values, inverse, inner):
    along = jnp.mean(values * inner, axis=-1, keepdims=True)
    return inverse * (inner - values * (inverse * inverse) * along)


def per_device(
    inputs,
    output_grad,
    source_tags,
    source_counts,
    gain_in,
    w_query,
    w_key,
    w_value,
    kernel,
    mixing,
    gain_head,
    w_out,
    gain_mid,
    w_gate,
    w_up,
    w_down,
):
    seqs, seg, width = inputs.shape
    parts = lax.axis_size("seq")
    lanes = lax.axis_size("batch")
    place_seq = lax.axis_index("seq")
    place_batch = lax.axis_index("batch")
    length = seg * parts
    groups = H // (2 * parts)
    local = groups * 2 * DH
    own = w_query.shape[0]
    blocks = parts * lanes

    gains = jnp.stack([gain_in, gain_head, gain_mid]).astype(f32)
    gains = lax.dynamic_update_slice_in_dim(
        jnp.zeros((3, width), f32), gains, (place_batch * parts + place_seq) * own, 1
    )
    gains = all_sum(gains.reshape(-1, 128), ("seq",))
    joint = jnp.stack([w_query, w_key, w_value], axis=1).reshape(own, 3, parts, local)
    joint = joint.transpose(2, 0, 1, 3).reshape(parts, own, 3 * local)
    joint = seq_swap(joint).reshape(parts * own, 3 * local)
    all_gains = all_sum(gains, ("batch",))
    hops = []
    x_all = [seq_gather(inputs[0], hops)]
    order = [
        (index, (index % lanes) * parts + index // lanes) for index in range(blocks)
    ]
    out_rows = lax.ppermute(w_out, ("batch", "seq"), order)
    joint = after(joint, all_gains, hops[0], out_rows)
    w_joint = batch_gather(joint)
    all_gains = all_gains.reshape(3, 1, width)
    gain_in32, gain_head32, gain_mid32 = all_gains[0], all_gains[1], all_gains[2]
    gain_own = lax.dynamic_slice_in_dim(gain_head32, place_seq * local, local, 1)
    kern_own = lax.dynamic_slice_in_dim(
        kernel.reshape(-1), place_seq * (2 * groups * QUERY_TAPS * KEY_TAPS), 2 * groups * QUERY_TAPS * KEY_TAPS, 0
    )
    mix_own = lax.dynamic_slice_in_dim(mixing.reshape(-1), place_seq * 4 * groups, 4 * groups, 0)

    w_join = batch_gather(out_rows)
    w_gate_up = batch_gather(jnp.concatenate([w_gate, w_up], axis=1))
    w_down_t = batch_gather(w_down.T)
    hidden_width = w_gate.shape[1]
    o_all = [lax.all_gather(output_grad[index], "seq", axis=0, tiled=True) for index in range(seqs)]

    source_ids = jnp.arange(source_counts.shape[0], dtype=jnp.int32)
    tag_count = jnp.sum(
        jnp.where(source_tags[:, None] == source_ids[None, :], source_counts[None, :], 0), axis=1
    )
    factor = length / tag_count.astype(f32)

    outputs, input_grads = [], []
    keep = []
    for index in range(seqs):
        if index:
            x_all.append(seq_gather(after(inputs[index], hops[-2]), gates=qkv))
        x32 = x_all[index].astype(f32)
        x_inverse = inverse_rms(x32)
        normed = (x32 * x_inverse * gain_in32).astype(bf16)
        qkv = nn(normed, w_joint).astype(bf16)[None]
        joined, heads, probs = attend_fwd(kern_own, mix_own, qkv, gain_own)
        middle = inputs[index].astype(f32) + seq_scatter(nn(joined[0], w_join).astype(bf16))
        keep.append([x_inverse, normed, qkv, joined, heads, probs, middle])
    gain_mid_grad = jnp.zeros((1, width), f32)
    gain_in_grad = jnp.zeros((1, width), f32)
    ffn = []
    results = []
    n_all = []
    scattered = []
    gate_by = []
    mid_inverses = []
    for index in range(seqs):
        middle = keep[index][-1]
        mid_inverses.append(inverse_rms(middle))
        n_own = (middle * mid_inverses[-1] * gain_mid32).astype(bf16)
        n_all.append(seq_gather(n_own, gates=gate_by[-1] if gate_by else None))
        whole = after(n_all[index], ffn[-1][4]) if ffn else n_all[index]
        both = nn(whole, w_gate_up)
        gate_by.append(both)
        gate, upward = both[:, :hidden_width], both[:, hidden_width:]
        sigma = 1.0 / (1.0 + jnp.exp(-gate))
        silu = gate * sigma
        hidden = (silu * upward).astype(bf16)
        o_here = after(o_all[index], scattered[-1][0]) if scattered else o_all[index]
        down_in = (o_here.astype(f32) * factor[index]).astype(bf16)
        hidden_grad = nn(down_in, w_down_t)
        gate_grad = (hidden_grad * upward * (sigma * (1.0 + gate * (1.0 - sigma)))).astype(bf16)
        up_grad = (hidden_grad * silu).astype(bf16)
        grads = lax.optimization_barrier(jnp.concatenate([gate_grad, up_grad], axis=1))
        mid_part = nt(after(grads, scattered[-1][1]) if scattered else grads, w_gate_up)
        mid_part = mid_part.astype(bf16)
        ffn.append((n_all[index], hidden, down_in, grads, mid_part))
        scattered.append([])
        scattered[-1].append(seq_scatter(mid_part, scattered[-1]))
    cat = lambda place: jnp.concatenate([item[place] for item in ffn], axis=0)
    all_hidden, all_down = cat(1), cat(2)
    g_gate_up = sum(tn(item[0], item[3]) for item in ffn).astype(bf16)
    g_down_t = tn(after(all_down, g_gate_up, scattered[-1][0]), all_hidden).astype(bf16)
    outers = []
    for index in range(seqs):
        middle, mid_inverse = keep[index][-1], mid_inverses[index]
        mid_grad = after(scattered[index][-1], g_down_t if index else g_gate_up)
        unit = middle * mid_inverse
        gain_mid_grad = gain_mid_grad + jnp.sum(mid_grad * unit, axis=0, keepdims=True)
        cotangent = output_grad[index].astype(f32) * factor[index]
        middle_grad = cotangent + rms_back(middle, mid_inverse, mid_grad * gain_mid32)
        a_all = seq_gather(middle_grad.astype(bf16), gates=outers[-1] if outers else None)
        outers.append(nt(a_all, w_join))
        keep[index] += [middle_grad, a_all]
    g_gate_up = batch_scatter(g_gate_up)
    g_down_t = batch_scatter(g_down_t)
    parts_out = [nt(item[1], w_down_t).astype(bf16).reshape(parts, seg, width) for item in ffn]
    parts_out = jnp.concatenate(parts_out, axis=1).reshape(parts * seqs * seg, width)
    parts_out = after(parts_out, outers[0])
    results = lax.psum_scatter(parts_out, "seq", scatter_dimension=0, tiled=True)
    results = results.reshape(seqs, seg, width)
    back = []
    for index in range(seqs):
        x_inverse, normed, qkv, joined, heads, probs, middle, middle_grad, a_all = keep[index]
        outer = outers[index][None]
        outer = after(outer, n_part, g_gate_up) if back else outer
        dqkv, corr, mix_sum, head_sum = attend_bwd(
            kern_own, mix_own, qkv, gain_own, heads, probs, outer
        )
        n_part = nt(after(dqkv, g_down_t)[0] if back else dqkv[0], w_joint)
        unit_all = x_all[index].astype(f32) * x_inverse
        gain_in_grad = gain_in_grad + jnp.sum(n_part * unit_all, axis=0, keepdims=True)
        n_grad = seq_scatter(n_part.astype(bf16))
        x32 = inputs[index].astype(f32)
        inner = rms_back(x32, inverse_rms(x32), n_grad * gain_in32)
        input_grads.append((middle_grad + inner).astype(bf16))
        back.append((normed, dqkv[0], joined[0], a_all, corr, mix_sum, head_sum))
    cat = lambda place: jnp.concatenate([item[place] for item in back], axis=0)
    all_normed, all_dqkv, all_joined, all_a = cat(0), cat(1), cat(2), cat(3)
    g_joint = tn(all_normed, all_dqkv).astype(bf16)
    for index in range(seqs):
        middle = after(keep[index][6], back[-1][1])
        outputs.append((middle + results[index].astype(f32)).astype(bf16))
    g_out = tn(all_joined, all_a).astype(bf16)
    span = parts * own
    packed = [g_joint.reshape(lanes, span, 3 * local), g_out.reshape(lanes, -1, 3 * local)]
    packed = batch_scatter(jnp.concatenate(packed, axis=1).reshape(-1, 3 * local))
    g_out = packed[span:].reshape(own, width)
    g_out = lax.ppermute(g_out, ("batch", "seq"), [(there, here) for here, there in order])
    g_out = g_out.astype(f32)
    g_joint = seq_swap(packed[:span].reshape(parts, own, 3 * local)).astype(f32)
    g_joint = g_joint.reshape(parts, own, 3, local).transpose(2, 1, 0, 3).reshape(3, own, width)

    corr = sum(item[4] for item in back)
    mix_sum = sum(item[5] for item in back)
    head_sum = sum(item[6] for item in back)
    taps = corr[:, :KEY_TAPS].reshape(2 * groups, KEY_TAPS, QUERY_TAPS, TILE)
    kern_grad = taps.sum(-1).transpose(0, 2, 1)
    mix_grad = mix_sum[0, : 4 * groups]
    head_grad = head_sum[0]

    def spread(value, total):
        return lax.dynamic_update_slice_in_dim(
            jnp.zeros((total,), f32), value.reshape(-1), place_seq * value.size, 0
        )

    small = jnp.concatenate(
        [
            gain_in_grad[0],
            gain_mid_grad[0],
            spread(head_grad, width),
            spread(kern_grad, H * QUERY_TAPS * KEY_TAPS),
            spread(mix_grad, H * 2),
        ]
    )
    size = small.size
    small = jnp.pad(small, (0, -size % 1024)).reshape(-1, 128)
    small = all_sum(small).reshape(-1)
    start = (place_batch * parts + place_seq) * own
    cuts = [lax.dynamic_slice_in_dim(small, start + step * width, own, 0) for step in range(3)]
    kernel_sum = small[3 * width : 3 * width + H * QUERY_TAPS * KEY_TAPS].reshape(kernel.shape)
    mixing_sum = small[3 * width + H * QUERY_TAPS * KEY_TAPS : size].reshape(mixing.shape)
    return (
        jnp.stack(outputs),
        jnp.stack(input_grads),
        cuts[0],
        g_joint[0],
        g_joint[1],
        g_joint[2],
        kernel_sum,
        mixing_sum,
        cuts[2],
        g_out,
        cuts[1],
        g_gate_up[:, :hidden_width].astype(f32),
        g_gate_up[:, hidden_width:].astype(f32),
        g_down_t.T.astype(f32),
    )


def solution(mesh):
    rows = P(("batch", "seq"))
    mats = P(("batch", "seq"), None)
    tokens = P("batch", "seq", None)
    in_specs = (
        tokens,
        tokens,
        P("batch"),
        P(),
        rows,
        mats,
        mats,
        mats,
        P(),
        P(),
        rows,
        mats,
        rows,
        P("batch", "seq"),
        P("batch", "seq"),
        P("seq", "batch"),
    )
    out_specs = (
        tokens,
        tokens,
        rows,
        mats,
        mats,
        mats,
        P(),
        P(),
        rows,
        mats,
        rows,
        P("batch", "seq"),
        P("batch", "seq"),
        P("seq", "batch"),
    )
    return jax.shard_map(
        per_device, mesh=mesh, in_specs=in_specs, out_specs=out_specs, check_vma=False
    )
```
